32 devices in a mesh: groups: 2 (over y), fsdp: 4 (over z), dp: 4 (over x, core).
Axes of the slice: x: 2, y: 2, z: 4, core: 2. Of those that a mesh axis runs over, the one named last changes fastest.
Arguments:
- hidden_in: bfloat16 [4096, 8192], P(('groups', 'dp'), 'fsdp'), parts along dimension 0, may hold values from -6 to 6
- cotangent: bfloat16 [4096, 9216], P(('groups', 'dp'), 'fsdp'), parts along dimension 0, may hold values from -6 to 6
- base_codes: bfloat16 [8192, 9216], P('fsdp', 'dp'), may hold values from -1 to 1
- base_scales: bfloat16 [8192, 144], P('fsdp', 'dp'), may hold values from 0.0079956055 to 0.039794922
- factor_a: bfloat16 [32, 131072], P('groups', 'fsdp'), parts along dimension 0, may hold values from -0.0625 to 0.0625
- factor_b: bfloat16 [32, 73728], P('groups', 'fsdp'), parts along dimension 0, may hold values from -0.0625 to 0.0625
- task_state: bfloat16 [32, 512], P('groups', 'dp'), parts along dimension 0, may hold values from -0.1796875 to 0.1796875
- head_a: bfloat16 [512, 131072], P('dp', 'fsdp'), may hold values from -0.0004196167 to 0.0004196167
- head_b: bfloat16 [512, 73728], P('dp', 'fsdp'), may hold values from -0.0004196167 to 0.0004196167
- task_ids: int32 [8], P(('groups', 'dp')), parts along dimension 0, may hold values from 0 to 15
- valid_counts: int32 [8], P(('groups', 'dp')), parts along dimension 0, may hold values from 64 to 384, as said below
- owners: int32 [32], P('groups'), parts along dimension 0, may hold values from 0 to 3, as said below
Outputs:
- input_gradient: bfloat16 [4096, 8192], P(('groups', 'dp'), 'fsdp'), parts along dimension 0
- grad_head_a: float32 [1024, 131072], P(('groups', 'dp'), 'fsdp'), parts along dimension 0
- grad_head_b: float32 [1024, 73728], P(('groups', 'dp'), 'fsdp'), parts along dimension 0
- grad_state: float32 [32, 512], P(('groups', 'fsdp'), 'dp'), parts along dimension 0
The draws below stay inside these ranges and needn't reach their ends.
There are 2 independent parts, one for each index of `groups`. The reference program is written for one: setup_inputs(seed, part) draws one part's arguments, and reference() takes and returns one part's arrays. A program takes and returns all parts, laid end to end along the dimension named above; an argument that names none is the same for every part. Nothing has to cross between parts.
Inputs may be any that keep to these rules, and one draw needn't show every extreme that they name: `valid_counts`: every sequence has at most 384 valid tokens, and some sequence has exactly 384. `owners`: no owner has more than 4 tasks, and some owner has exactly 4.
All inputs are finite; a program needn't handle non-finite values.
Results may differ from the reference program's by a relative error of at most 0.017.
Values may be sent and summed in bfloat16 or wider, within the bound.
No kernel may reach another device: no remote copies, remote signals or barrier semaphores. Data moves between devices by JAX's collectives and lax.ppermute only.
A program may use at most 320 MiB of HBM per device.

```python
import math
import jax
import jax.numpy as jnp
from jax import lax

MODEL_WIDTH = 8192
HEADS = 64
KV_HEADS = 8
HEAD_DIM = 128
ADAPTER_RANK = 8
QBLOCK = 64
HD = 512
TASKS = 16
SLOTS = 4
SEQ = 512
LIVE = 384
QUERY_VALUE_COLS = 9216
SEQS = 4
TOKENS = 2048
N_FSDP = 4
N_DP = 4


def draw_valid_counts(key, part):
    first_key, second_key = jax.random.split(jax.random.fold_in(key, 11))
    counts = jax.random.randint(first_key, (SEQS,), SEQ // 8, LIVE + 1)
    longest = jax.random.randint(second_key, (), 0, SEQS)
    return jnp.where(jnp.arange(SEQS) == longest, LIVE, counts).astype(jnp.int32)


def draw_owners(key, part):
    first_key, second_key = jax.random.split(jax.random.fold_in(key, 23))
    task_order = jax.random.permutation(first_key, TASKS)
    owner_order = jax.random.permutation(second_key, N_FSDP)
    ranks = jnp.arange(TASKS)
    bucket = jnp.where(ranks < SLOTS, 0, 1 + (ranks - SLOTS) % (N_FSDP - 1))
    chosen = owner_order[bucket].astype(jnp.int32)
    return jnp.zeros((TASKS,), jnp.int32).at[task_order].set(chosen)


def set_ends(result, key, least, largest):
    place = [jax.random.randint(jax.random.fold_in(key, axis), (), 0, length) for axis, length in enumerate(result.shape)]
    widest = result.shape.index(max(result.shape))
    next_to = place[:widest] + [(place[widest] + 1) % result.shape[widest]] + place[widest + 1:]
    return result.at[tuple(place)].set(least).at[tuple(next_to)].set(largest)


def shard_levels(stream_key, extent, pieces, least, largest):
    level, own = 1.0, jax.random.fold_in(stream_key, 6)
    for position, parts in pieces:
        steps = jnp.exp(jax.random.uniform(jax.random.fold_in(own, position), (parts,), jnp.float32, least / len(pieces), largest / len(pieces)))
        level = level * jnp.repeat(steps, extent[position] // parts).reshape([-1 if axis == position else 1 for axis in range(len(extent))])
    return level


def bell_draw(key, dims, deviation, reach, cuts=(), kind=jnp.bfloat16):
    array = jax.random.normal(key, dims, jnp.float32) * deviation
    if len(cuts) > 0:
        array = shard_levels(key, dims, cuts, -0.22, 0.18) * array
    return jnp.clip(array, min=-reach, max=reach).astype(kind)


def setup_inputs(seed: int = 0, part: int = 0) -> dict:
    arg_keys = jax.random.split(jax.random.key(seed), 13)
    part_splits = jax.random.split(jax.random.fold_in(arg_keys[12], part), 13)
    hidden_in = bell_draw(part_splits[0], (TOKENS, MODEL_WIDTH), 1.0, 6.0, ((0, 4), (1, 4)))
    cotangent = bell_draw(part_splits[1], (TOKENS, QUERY_VALUE_COLS), 1.0, 6.0, ((0, 4), (1, 4)))
    base_codes = jnp.clip(jax.random.uniform(arg_keys[2], (MODEL_WIDTH, QUERY_VALUE_COLS), jnp.float32, -1.0, 1.0) * shard_levels(arg_keys[2], (MODEL_WIDTH, QUERY_VALUE_COLS), ((0, 4), (1, 4)), -0.4, 0.0), -1.0, 1.0).astype(jnp.bfloat16)
    base_scales = jnp.clip(jnp.exp(math.log(0.039794922) - 1.6048472 * jax.random.uniform(arg_keys[3], (MODEL_WIDTH, QUERY_VALUE_COLS // QBLOCK), jnp.float32) ** shard_levels(arg_keys[3], (MODEL_WIDTH, QUERY_VALUE_COLS // QBLOCK), ((0, 4), (1, 4)), -0.2, 0.2)), 0.0079956055, 0.039794922).astype(jnp.bfloat16)
    factor_a = bell_draw(part_splits[4], (TASKS, MODEL_WIDTH * 2 * ADAPTER_RANK), MODEL_WIDTH ** -0.5, 0.0625, ((1, 4),))
    factor_b = bell_draw(part_splits[5], (TASKS, QUERY_VALUE_COLS * ADAPTER_RANK), QUERY_VALUE_COLS ** -0.5, 0.0625, ((1, 4),))
    task_state = bell_draw(part_splits[6], (TASKS, HD), 0.03, 0.1796875, ((1, 4),))
    head_a = bell_draw(arg_keys[7], (HD, MODEL_WIDTH * 2 * ADAPTER_RANK), 0.00007, 0.0004196167, ((0, 4), (1, 4)))
    head_b = bell_draw(arg_keys[8], (HD, QUERY_VALUE_COLS * ADAPTER_RANK), 0.00007, 0.0004196167, ((0, 4), (1, 4)))
    task_ids = set_ends(jax.random.randint(part_splits[9], (SEQS,), 0, TASKS), jax.random.fold_in(part_splits[9], 1), 0, TASKS - 1).astype(jnp.int32)
    valid_counts = draw_valid_counts(jax.random.fold_in(jax.random.fold_in(arg_keys[12], part), 71), part)
    owners = draw_owners(jax.random.fold_in(jax.random.fold_in(arg_keys[12], part), 71), part)
    return dict(hidden_in=hidden_in, cotangent=cotangent, base_codes=base_codes, base_scales=base_scales, factor_a=factor_a, factor_b=factor_b, task_state=task_state, head_a=head_a, head_b=head_b, task_ids=task_ids, valid_counts=valid_counts, owners=owners)


adapter_scale = 2.0


def reference(hidden_in, cotangent, base_codes, base_scales, factor_a, factor_b, task_state, head_a, head_b, task_ids, valid_counts, owners):
    highest = lax.Precision.HIGHEST
    sequence_count = N_DP
    positions = jnp.arange(SEQ, dtype=jnp.int32)
    row_keep = (positions[None, :] < valid_counts[:, None]).reshape(SEQ * sequence_count, 1)
    masked = cotangent * row_keep.astype(jnp.bfloat16)
    block_count = base_scales.shape[1]
    weight = (base_codes.astype(jnp.float32).reshape(MODEL_WIDTH, block_count, QBLOCK) * base_scales.astype(jnp.float32)[:, :, None]).reshape(MODEL_WIDTH, QUERY_VALUE_COLS).astype(jnp.bfloat16)
    task_table = jnp.arange(TASKS, dtype=jnp.int32)
    one_hot = (task_ids[:, None] == task_table[None, :]).astype(jnp.float32)
    chosen_a = factor_a[task_ids].astype(jnp.float32).reshape(sequence_count, MODEL_WIDTH, 2 * ADAPTER_RANK)
    chosen_b = factor_b[task_ids].astype(jnp.float32).reshape(sequence_count, QUERY_VALUE_COLS, ADAPTER_RANK)
    group_cols = (HEADS // KV_HEADS + 1) * HEAD_DIM
    value_column_start = ((jnp.arange(QUERY_VALUE_COLS, dtype=jnp.int32) % group_cols) >= (HEADS // KV_HEADS) * HEAD_DIM)[None, :, None]
    empty_b = jnp.zeros_like(chosen_b)
    joined_b = jnp.concatenate([jnp.where(value_column_start, empty_b, chosen_b), jnp.where(value_column_start, chosen_b, empty_b)], axis=2)
    widened_input = hidden_in.astype(jnp.float32).reshape(sequence_count, SEQ, MODEL_WIDTH)
    grads_wide = masked.astype(jnp.float32).reshape(sequence_count, SEQ, QUERY_VALUE_COLS)
    lowrank_in = jnp.einsum('bsd,bdr->bsr', widened_input, chosen_a)
    lowrank_low = lax.optimization_barrier(lowrank_in.astype(jnp.bfloat16)).astype(jnp.float32)
    lowrank_out = jnp.einsum('bsn,bnr->bsr', grads_wide, joined_b)
    reduced_rank_gradient = lax.optimization_barrier(lowrank_out.astype(jnp.bfloat16)).astype(jnp.float32)
    frozen_gradient = jnp.dot(masked.astype(jnp.float32), weight.astype(jnp.float32).T, precision=highest)
    adapter_contribution = jnp.einsum('bsr,bdr->bsd', reduced_rank_gradient, chosen_a).reshape(sequence_count * SEQ, MODEL_WIDTH)
    input_gradient = (frozen_gradient + adapter_scale * adapter_contribution).astype(jnp.bfloat16)
    down_gradient = adapter_scale * jnp.einsum('ftg,ftx->fgx', widened_input, reduced_rank_gradient).reshape(sequence_count, MODEL_WIDTH * 2 * ADAPTER_RANK)
    mixed_products = jnp.einsum('bsn,bsr->bnr', grads_wide, lowrank_low)
    up_gradient = adapter_scale * jnp.where(value_column_start, mixed_products[:, :, ADAPTER_RANK:], mixed_products[:, :, :ADAPTER_RANK]).reshape(sequence_count, QUERY_VALUE_COLS * ADAPTER_RANK)
    sum_down = jnp.dot(one_hot.T, down_gradient, precision=highest)
    sum_up = jnp.dot(one_hot.T, up_gradient, precision=highest)
    state_wide = task_state.astype(jnp.float32)
    grad_head_a = jnp.dot(state_wide.T, sum_down, precision=highest)
    grad_head_b = jnp.dot(state_wide.T, sum_up, precision=highest)
    state_grad = jnp.dot(sum_down, head_a.astype(jnp.float32).T, precision=highest) + jnp.dot(sum_up, head_b.astype(jnp.float32).T, precision=highest)
    same_owner = owners[:, None] == owners[None, :]
    earlier = task_table[None, :] < task_table[:, None]
    slot_index = jnp.sum((same_owner & earlier).astype(jnp.int32), axis=1)
    target = (owners * SLOTS + slot_index).astype(jnp.int32)
    grad_state = jnp.zeros((SLOTS * N_FSDP, HD), jnp.float32).at[target].add(state_grad)
    return (input_gradient, grad_head_a, grad_head_b, grad_state)
```

```python
import jax
import jax.numpy as jnp
from jax import lax
from jax.experimental import pallas as pl
from jax.experimental.pallas import tpu as pltpu
from jax.sharding import PartitionSpec as P

HEADS = 64
KV_HEADS = 8
HEAD_DIM = 128
QBLOCK = 64
SLOTS = 4
LIVE = 384
TILE = 256

adapter_scale = 2.0


def dequantize(codes, scales):
    cols, blocks = codes.shape[1], scales.shape[1]
    spread = (
        lax.broadcasted_iota(jnp.int32, (blocks, cols), 1) // QBLOCK
        == lax.broadcasted_iota(jnp.int32, (blocks, cols), 0)
    ).astype(jnp.bfloat16)
    wide = jnp.dot(scales, spread, preferred_element_type=jnp.float32)
    return (codes.astype(jnp.float32) * wide).astype(jnp.bfloat16)


def after(value, *done):
    return lax.optimization_barrier((value, done))[0]


def input_gradient_kernel(tiles, where, count, *refs):
    meta, low, chosen = refs[:3]
    near = refs[3:10]
    arrays = refs[10 : 10 + count]
    out, cot, wbuf, csem, wsem = refs[10 + count :]
    weights = [arrays[index].at[pl.ds(offset * TILE, TILE)] for index, offset in where]
    z, p, y, valid = meta[0], meta[1], meta[2], meta[3]
    own, up1, dn1, up2, dn2, up3, dn3 = near
    depth = wbuf.shape[0]
    steps = 4 * tiles

    def fetch(step, slot):
        for index in range(steps):

            @pl.when(step == index)
            def _():
                pltpu.make_async_copy(weights[index], wbuf.at[slot], wsem.at[slot]).start()

    def place(first, second, take_first, slot):
        @pl.when(take_first)
        def _():
            pltpu.make_async_copy(first, cot.at[slot], csem.at[slot]).start()

        @pl.when(jnp.logical_not(take_first))
        def _():
            pltpu.make_async_copy(second, cot.at[slot], csem.at[slot]).start()

    pltpu.make_async_copy(own, cot.at[0], csem.at[0]).start()
    place(up1, dn3, z >= 1, 1)
    place(up2, dn2, z >= 2, 2)
    place(up3, dn1, z >= 3, 3)
    for slot in range(depth - 1):
        pltpu.make_async_copy(weights[slot], wbuf.at[slot], wsem.at[slot]).start()
    for slot in range(4):
        pltpu.make_async_copy(own, cot.at[slot], csem.at[slot]).wait()
    keep = lax.broadcasted_iota(jnp.int32, (LIVE, 1), 0) < valid
    out[LIVE:, :] = jnp.zeros((out.shape[0] - LIVE, out.shape[1]), out.dtype)

    @pl.loop(0, tiles)
    def _(tile):
        half = (tiles - 2) // 2
        first = tile + jnp.where(tile < half, y * half, -y * half)
        place_at = jnp.where(tile < 2 * half, first, tile)
        start = pl.multiple_of(place_at * TILE, TILE)
        acc = adapter_scale * lax.dot_general(
            low[...],
            chosen[pl.ds(start, TILE), :],
            (((1,), (1,)), ((), ())),
            preferred_element_type=jnp.float32,
        )
        total = jnp.zeros((LIVE, TILE), jnp.float32)
        for j in range(4):
            step = tile * 4 + j
            slot = lax.rem(step, depth)
            ahead = step + depth - 1
            fetch(ahead, lax.rem(ahead, depth))
            pltpu.make_async_copy(weights[0], wbuf.at[slot], wsem.at[slot]).wait()
            block = jnp.bitwise_and(z - jnp.bitwise_xor(p, j), 3)
            total = total + lax.dot_general(
                cot[block],
                wbuf[slot],
                (((1,), (1,)), ((), ())),
                preferred_element_type=jnp.float32,
            )
        result = jnp.where(keep, total, 0.0) + acc
        out[:LIVE, pl.ds(start, TILE)] = result.astype(out.dtype)


def permute_plan(own, codes, scales, y):
    rows = codes.shape[0]
    tiles = rows // TILE
    half = (tiles - 2) // 2
    up = lambda step: [(i, i + 1) for i in range(step, 3)]
    down = lambda step: [(i + 1, i) for i in range(0, 3 - step)]
    across = lambda v: lax.ppermute(v, "dp", [(i, i ^ 2) for i in range(4)])
    core = lambda v: lax.ppermute(v, "dp", [(i, i ^ 1) for i in range(4)])
    over = lambda v: lax.ppermute(v, "groups", [(0, 1), (1, 0)])

    def part(start, size):
        return dequantize(
            lax.dynamic_slice_in_dim(codes, start, size, 0),
            lax.dynamic_slice_in_dim(scales, start, size, 0),
        )

    up1 = lax.ppermute(own, "fsdp", up(0))
    dn1 = lax.ppermute(own, "fsdp", down(0))
    near_tiles = [part((y * half + i) * TILE, TILE) for i in range(half)]
    last_tiles = [part((2 * half + i) * TILE, TILE) for i in range(2)]
    middle = part((1 - y) * half * TILE, half * TILE)
    m0, m1, m2 = near_tiles
    e0, e1 = last_tiles
    x0 = across(m0)
    x1 = across(m1)
    sib_middle = core(middle)
    sib0 = core(after(m0, sib_middle))
    sib1 = core(after(m1, sib0))
    sib2 = core(after(m2, sib1))
    y0 = over(after(x0, sib2))
    x2 = across(after(m2, x0))
    up2 = lax.ppermute(after(up1, x0), "fsdp", up(1))
    dn2 = lax.ppermute(after(dn1, x0), "fsdp", down(1))
    y1 = over(after(x1, up1, dn1))
    fx0 = core(after(x0, x1, y0))
    fy0 = core(after(y0, fx0))
    sib3 = core(after(e0, fy0))
    sib4 = core(after(e1, sib3))
    x3 = across(after(e0, sib4))
    y2 = over(after(x2, sib4))
    fx1 = core(after(x1, x2))
    fy1 = core(after(y1, fx1))
    fx2 = core(after(x2, fy1))
    up3 = lax.ppermute(after(up2, x2), "fsdp", up(2))
    dn3 = lax.ppermute(after(dn2, x2), "fsdp", down(2))
    x4 = across(after(e1, fx2))
    fx3 = core(after(x3, up2, dn2))
    fy2 = core(after(y2, fx3))
    fx4 = core(x4)
    mine = [(m0, 0), (m1, 0), (m2, 0), (middle, 0), (middle, 1), (middle, 2), (e0, 0), (e1, 0)]
    sibling = [(sib0, 0), (sib1, 0), (sib2, 0), (sib_middle, 0), (sib_middle, 1), (sib_middle, 2)]
    sibling += [(sib3, 0), (sib4, 0)]
    far = [(v, 0) for v in (x0, x1, x2, y0, y1, y2, x3, x4)]
    far_sibling = [(v, 0) for v in (fx0, fx1, fx2, fy0, fy1, fy2, fx3, fx4)]
    places = []
    for i in range(tiles):
        places += [mine[i], sibling[i], far[i], far_sibling[i]]
    arrays = []
    for array, _ in places:
        if not any(array is other for other in arrays):
            arrays.append(array)
    where = [
        ([array is other for other in arrays].index(True), offset) for array, offset in places
    ]
    near = [own, up1, dn1, up2, dn2, up3, dn3]
    return near, arrays, where, tiles, (up1, dn1)


def shards(
    hidden_in,
    cotangent,
    base_codes,
    base_scales,
    factor_a,
    factor_b,
    task_state,
    head_a,
    head_b,
    task_ids,
    valid_counts,
    owners,
):
    f32, bf16 = jnp.float32, jnp.bfloat16
    n_groups, n_fsdp, n_dp = (lax.axis_size(a) for a in ("groups", "fsdp", "dp"))
    z, p, y = (lax.axis_index(a) for a in ("fsdp", "dp", "groups"))
    seq_len, width_part = hidden_in.shape
    tasks_all, factor_cols = factor_a.shape
    rank_double = factor_cols // width_part
    rank_half = rank_double // 2
    joined_part = cotangent.shape[1]
    joined_part_w = base_codes.shape[1]
    hidden = hidden_in[:LIVE]
    own = cotangent[:LIVE]
    lines = (n_groups, n_fsdp, n_dp) == (2, 4, 4) and width_part == 8 * TILE
    if lines:
        near, arrays, where, tiles, first = permute_plan(own, base_codes, base_scales, y)

    task = task_ids[0]
    chosen_a = lax.dynamic_slice_in_dim(factor_a, task, 1, 0).reshape(width_part, rank_double)
    chosen_b = lax.dynamic_slice_in_dim(factor_b, task, 1, 0).reshape(joined_part, rank_half)
    group_cols = (HEADS // KV_HEADS + 1) * HEAD_DIM
    columns = z * joined_part + lax.broadcasted_iota(jnp.int32, (joined_part, 1), 0)
    value_column = columns % group_cols >= HEADS // KV_HEADS * HEAD_DIM
    empty_b = jnp.zeros_like(chosen_b)
    joined_b = jnp.concatenate(
        [jnp.where(value_column, empty_b, chosen_b), jnp.where(value_column, chosen_b, empty_b)],
        axis=1,
    )
    inner_part = jnp.dot(hidden, chosen_a, preferred_element_type=f32)
    outer_part = jnp.dot(own, joined_b, preferred_element_type=f32)
    parts = jnp.concatenate([inner_part, outer_part], axis=1).astype(bf16)
    sums = jnp.sum(lax.all_gather(parts, "fsdp", axis=0).astype(f32), axis=0)
    keep = lax.broadcasted_iota(jnp.int32, (LIVE, 1), 0) < valid_counts[0]
    sums = jnp.where(keep, sums, 0.0).astype(bf16)
    low_in, low_grad = sums[:, :rank_double], sums[:, rank_double:]

    down_gradient = adapter_scale * lax.dot_general(
        hidden, low_grad, (((0,), (0,)), ((), ())), preferred_element_type=f32
    )
    mixed = lax.dot_general(own, low_in, (((0,), (0,)), ((), ())), preferred_element_type=f32)
    up_gradient = adapter_scale * jnp.where(value_column, mixed[:, rank_half:], mixed[:, :rank_half])
    down_cols = width_part * rank_double
    up_cols = joined_part * rank_half
    row = jnp.concatenate(
        [
            down_gradient.astype(bf16).reshape(1, down_cols),
            up_gradient.astype(bf16).reshape(1, up_cols),
            jnp.full((1, 128), task, f32).astype(bf16),
        ],
        axis=1,
    )
    if lines:
        row = after(row, *first)
    rows = lax.all_gather(row, "dp", axis=0, tiled=True)
    ids = rows[:, down_cols + up_cols].astype(jnp.int32)
    rows_down, rows_up = rows[:, :down_cols], rows[:, down_cols : down_cols + up_cols]
    one_hot = ids[:, None] == lax.broadcasted_iota(jnp.int32, (1, tasks_all), 1)
    states = jnp.dot(one_hot.astype(bf16), task_state, preferred_element_type=f32).astype(bf16)
    grad_head_a = lax.dot_general(
        states, rows_down, (((0,), (0,)), ((), ())), preferred_element_type=f32
    )
    grad_head_b = lax.dot_general(
        states, rows_up, (((0,), (0,)), ((), ())), preferred_element_type=f32
    )
    state_part = lax.dot_general(
        rows_down, head_a, (((1,), (1,)), ((), ())), preferred_element_type=f32
    ) + lax.dot_general(rows_up, head_b, (((1,), (1,)), ((), ())), preferred_element_type=f32)
    state_sum = jnp.sum(lax.all_gather(state_part, "fsdp", axis=0), axis=0)
    task_rows = lax.broadcasted_iota(jnp.int32, (tasks_all, tasks_all), 0)
    task_other = lax.broadcasted_iota(jnp.int32, (tasks_all, tasks_all), 1)
    same_owner = owners[:, None] == owners[None, :]
    slot_index = jnp.sum((same_owner & (task_other < task_rows)).astype(jnp.int32), axis=1)
    target = owners * SLOTS + slot_index
    seq_target = jnp.sum(jnp.where(one_hot, target[None, :], 0), axis=1)
    own_rows = z * SLOTS + lax.broadcasted_iota(jnp.int32, (SLOTS, 1), 0)
    selector = (own_rows == seq_target[None, :]).astype(f32)
    grad_state = jnp.sum(selector[:, :, None] * state_sum[None, :, :], axis=1)

    if lines:
        meta = jnp.stack([z, p, y, valid_counts[0]]).astype(jnp.int32)
        any_spec = pl.BlockSpec(memory_space=pl.ANY)
        vmem_spec = pl.BlockSpec(memory_space=pltpu.VMEM)
        depth = 4
        input_gradient = pl.pallas_call(
            lambda *refs: input_gradient_kernel(tiles, where, len(arrays), *refs),
            out_shape=jax.ShapeDtypeStruct((seq_len, width_part), bf16),
            in_specs=[pl.BlockSpec(memory_space=pltpu.SMEM), vmem_spec, vmem_spec]
            + [any_spec] * (len(near) + len(arrays)),
            out_specs=vmem_spec,
            scratch_shapes=[
                pltpu.VMEM((4, LIVE, joined_part), bf16),
                pltpu.VMEM((depth, TILE, joined_part_w), bf16),
                pltpu.SemaphoreType.DMA((4,)),
                pltpu.SemaphoreType.DMA((depth,)),
            ],
            compiler_params=pltpu.CompilerParams(vmem_limit_bytes=40 * 2**20),
        )(meta, low_grad, chosen_a, *near, *arrays)
    else:
        weight = dequantize(
            lax.all_gather(base_codes, "dp", axis=1, tiled=True),
            lax.all_gather(base_scales, "dp", axis=1, tiled=True),
        )
        merged = lax.dot_general(
            lax.all_gather(own, "fsdp", axis=1, tiled=True),
            weight,
            (((1,), (1,)), ((), ())),
            preferred_element_type=f32,
        )
        adapter = lax.dot_general(
            low_grad, chosen_a, (((1,), (1,)), ((), ())), preferred_element_type=f32
        )
        live = (jnp.where(keep, merged, 0.0) + adapter_scale * adapter).astype(bf16)
        input_gradient = jnp.pad(live, ((0, seq_len - LIVE), (0, 0)))
    return (input_gradient, grad_head_a, grad_head_b, grad_state)


def solution(mesh):
    placed = (
        P(("groups", "dp"), "fsdp"),
        P(("groups", "dp"), "fsdp"),
        P("fsdp", "dp"),
        P("fsdp", "dp"),
        P("groups", "fsdp"),
        P("groups", "fsdp"),
        P("groups", "dp"),
        P("dp", "fsdp"),
        P("dp", "fsdp"),
        P(("groups", "dp")),
        P(("groups", "dp")),
        P("groups"),
    )
    return jax.shard_map(
        shards,
        mesh=mesh,
        in_specs=placed,
        out_specs=(
            P(("groups", "dp"), "fsdp"),
            P(("groups", "dp"), "fsdp"),
            P(("groups", "dp"), "fsdp"),
            P(("groups", "fsdp"), "dp"),
        ),
        check_vma=False,
    )
```

```python
import math

import jax
import jax.numpy as jnp
from jax import lax
from jax.experimental import pallas as pl
from jax.experimental.pallas import tpu as pltpu
from jax.sharding import PartitionSpec as P

HEADS = 64
KV_HEADS = 8
HEAD_DIM = 128
QBLOCK = 64
SLOTS = 4
LIVE = 384
TILE = 256

adapter_scale = 2.0


def dequantize(codes, scales):
    rows, cols = codes.shape
    blocks = scales.shape[1]
    return (
        (
            codes.astype(jnp.float32).reshape(rows, blocks, QBLOCK)
            * scales.astype(jnp.float32)[:, :, None]
        )
        .reshape(rows, cols)
        .astype(jnp.bfloat16)
    )


def weight_kernel(group, codes, scales, out):
    cols, blocks = codes.shape[1], scales.shape[0]
    spread = (
        lax.broadcasted_iota(jnp.int32, (cols, blocks), 0) // QBLOCK
        == lax.broadcasted_iota(jnp.int32, (cols, blocks), 1)
    ).astype(jnp.bfloat16)
    wide = jnp.dot(spread, scales[...], preferred_element_type=jnp.float32)
    out[0] = (jnp.transpose(codes[...]).astype(jnp.float32) * wide).astype(jnp.bfloat16)


def weight_tiles(group, codes, scales, first, count, half):
    cols, blocks = codes.shape[1], scales.shape[0]

    def place(i, group):
        at = first + i
        moved = jnp.where(at < half, at + group[0] * half, at - group[0] * half)
        return jnp.where(at < 2 * half, moved, at)

    return pl.pallas_call(
        weight_kernel,
        out_shape=jax.ShapeDtypeStruct((count, cols, TILE), jnp.bfloat16),
        grid_spec=pltpu.PrefetchScalarGridSpec(
            num_scalar_prefetch=1,
            grid=(count,),
            in_specs=[
                pl.BlockSpec((TILE, cols), lambda i, group: (place(i, group), 0)),
                pl.BlockSpec((blocks, TILE), lambda i, group: (0, place(i, group))),
            ],
            out_specs=pl.BlockSpec((1, cols, TILE), lambda i, group: (i, 0, 0)),
        ),
        compiler_params=pltpu.CompilerParams(vmem_limit_bytes=32 * 2**20),
        cost_estimate=pl.CostEstimate(flops=0, transcendentals=0, bytes_accessed=0),
    )(group, codes, scales)


def product_kernel(hidden, cotangent, chosen, joined, out):
    inner = jnp.dot(hidden[:LIVE, :], chosen[...], preferred_element_type=jnp.float32)
    outer = jnp.dot(cotangent[:LIVE, :], joined[...], preferred_element_type=jnp.float32)
    out[...] = jnp.concatenate([inner, outer], axis=1).astype(out.dtype)


def factor_kernel(hidden, cotangent, grad, low, down, up):
    contract = (((0,), (0,)), ((), ()))
    down[...] = adapter_scale * lax.dot_general(
        hidden[:LIVE, :], grad[...], contract, preferred_element_type=jnp.float32
    )
    up[...] = adapter_scale * lax.dot_general(
        cotangent[:LIVE, :], low[...], contract, preferred_element_type=jnp.float32
    )


def head_kernel(states, rows, head, grad, part):
    grad[...] = lax.dot_general(
        states[...], rows[...], (((0,), (0,)), ((), ())), preferred_element_type=jnp.float32
    )

    @pl.when(pl.program_id(0) == 0)
    def _():
        part[...] = jnp.zeros_like(part)

    part[...] += lax.dot_general(
        rows[...], head[...], (((1,), (1,)), ((), ())), preferred_element_type=jnp.float32
    )


def head_grads(states, rows, head, first, block):
    hidden_units, cols = head.shape
    sequences = rows.shape[0]
    return pl.pallas_call(
        head_kernel,
        out_shape=[
            jax.ShapeDtypeStruct((hidden_units, cols), jnp.float32),
            jax.ShapeDtypeStruct((sequences, hidden_units), jnp.float32),
        ],
        grid=(cols // block,),
        in_specs=[
            pl.BlockSpec((sequences, hidden_units), lambda i: (0, 0)),
            pl.BlockSpec((sequences, block), lambda i: (0, first // block + i)),
            pl.BlockSpec((hidden_units, block), lambda i: (0, i)),
        ],
        out_specs=[
            pl.BlockSpec((hidden_units, block), lambda i: (0, i)),
            pl.BlockSpec((sequences, hidden_units), lambda i: (0, 0)),
        ],
        compiler_params=pltpu.CompilerParams(vmem_limit_bytes=32 * 2**20),
        cost_estimate=pl.CostEstimate(flops=0, transcendentals=0, bytes_accessed=0),
    )(states, rows, head)


def whole_call(kernel, out_shape, *operands):
    spec = pl.BlockSpec(memory_space=pltpu.VMEM)
    return pl.pallas_call(
        kernel,
        out_shape=out_shape,
        in_specs=[spec] * len(operands),
        out_specs=jax.tree.map(lambda _: spec, out_shape),
        compiler_params=pltpu.CompilerParams(vmem_limit_bytes=32 * 2**20),
        cost_estimate=pl.CostEstimate(flops=0, transcendentals=0, bytes_accessed=0),
    )(*operands)


def after(value, *done):
    return lax.optimization_barrier((value, done))[0]


def input_gradient_kernel(tiles, where, count, *refs):
    meta, low, chosen = refs[:3]
    near = refs[3:10]
    arrays = refs[10 : 10 + count]
    out, cot, wbuf, csem, wsem = refs[10 + count :]
    weights = [arrays[index].at[offset] for index, offset in where]
    z, p, y, valid = meta[0], meta[1], meta[2], meta[3]
    own, up1, dn1, up2, dn2, up3, dn3 = near
    depth = wbuf.shape[0]
    steps = 4 * tiles

    def fetch(step, slot):
        for index in range(steps):

            @pl.when(step == index)
            def _():
                pltpu.make_async_copy(weights[index], wbuf.at[slot], wsem.at[slot]).start()

    def place(first, second, take_first, slot):
        @pl.when(take_first)
        def _():
            pltpu.make_async_copy(first, cot.at[slot], csem.at[slot]).start()

        @pl.when(jnp.logical_not(take_first))
        def _():
            pltpu.make_async_copy(second, cot.at[slot], csem.at[slot]).start()

    pltpu.make_async_copy(own, cot.at[0], csem.at[0]).start()
    place(up1, dn3, z >= 1, 1)
    place(up2, dn2, z >= 2, 2)
    place(up3, dn1, z >= 3, 3)
    for slot in range(depth - 1):
        pltpu.make_async_copy(weights[slot], wbuf.at[slot], wsem.at[slot]).start()
    for slot in range(4):
        pltpu.make_async_copy(own, cot.at[slot], csem.at[slot]).wait()
    keep = lax.broadcasted_iota(jnp.int32, (LIVE, 1), 0) < valid
    out[LIVE:, :] = jnp.zeros((out.shape[0] - LIVE, out.shape[1]), out.dtype)

    @pl.loop(0, tiles)
    def _(tile):
        half = (tiles - 2) // 2
        first = tile + jnp.where(tile < half, y * half, -y * half)
        place_at = jnp.where(tile < 2 * half, first, tile)
        start = pl.multiple_of(place_at * TILE, TILE)
        acc = adapter_scale * lax.dot_general(
            low[...],
            chosen[pl.ds(start, TILE), :],
            (((1,), (1,)), ((), ())),
            preferred_element_type=jnp.float32,
        )
        total = jnp.zeros((LIVE, TILE), jnp.float32)
        for j in range(4):
            step = tile * 4 + j
            slot = lax.rem(step, depth)
            ahead = step + depth - 1
            fetch(ahead, lax.rem(ahead, depth))
            pltpu.make_async_copy(weights[0], wbuf.at[slot], wsem.at[slot]).wait()
            block = jnp.bitwise_and(z - jnp.bitwise_xor(p, j), 3)
            total = total + lax.dot_general(
                cot[block],
                wbuf[slot],
                (((1,), (0,)), ((), ())),
                preferred_element_type=jnp.float32,
            )
        result = jnp.where(keep, total, 0.0) + acc
        out[:LIVE, pl.ds(start, TILE)] = result.astype(out.dtype)


def gather_kernel(*refs):
    inputs, out, sem = refs[:-2], refs[-2], refs[-1]
    for i, ref in enumerate(inputs):
        pltpu.make_async_copy(ref, out.at[pl.ds(i, 1)], sem.at[i]).start()
    for i, ref in enumerate(inputs):
        pltpu.make_async_copy(ref, out.at[pl.ds(i, 1)], sem.at[i]).wait()


def gather_tiles(tiles):
    spec = pl.BlockSpec(memory_space=pl.ANY)
    return pl.pallas_call(
        gather_kernel,
        out_shape=jax.ShapeDtypeStruct((len(tiles),) + tiles[0].shape[1:], tiles[0].dtype),
        in_specs=[spec] * len(tiles),
        out_specs=spec,
        scratch_shapes=[pltpu.SemaphoreType.DMA((len(tiles),))],
        cost_estimate=pl.CostEstimate(flops=0, transcendentals=0, bytes_accessed=0),
    )(*tiles)


def permute_plan(own, codes, scales, y):
    tiles = codes.shape[0] // TILE
    half = (tiles - 2) // 2
    up = lambda step: [(i, i + 1) for i in range(step, 3)]
    down = lambda step: [(i + 1, i) for i in range(0, 3 - step)]
    across = lambda v: lax.ppermute(v, "dp", [(i, i ^ 2) for i in range(4)])
    core = lambda v: lax.ppermute(v, "dp", [(i, i ^ 1) for i in range(4)])
    over = lambda v: lax.ppermute(v, "groups", [(0, 1), (1, 0)])
    group = y.astype(jnp.int32).reshape(1)
    columns = scales.T

    up1 = lax.ppermute(own, "fsdp", up(0))
    dn1 = lax.ppermute(own, "fsdp", down(0))
    head = weight_tiles(group, codes, columns, 0, 1, half)
    tail = weight_tiles(after(group, head), codes, columns, 1, tiles - 1, half)
    x0 = across(head)
    x1 = across(tail[0:1])
    sib_tail = core(tail)
    sib_head = core(after(head, sib_tail))
    y0 = over(x0)
    x2 = across(after(tail[1:2], sib_tail))

    def rest(row, done):
        up2 = lax.ppermute(after(up1, row), "fsdp", up(1))
        dn2 = lax.ppermute(after(dn1, row), "fsdp", down(1))
        y1 = over(after(x1, up1, dn1))
        x3 = across(after(tail[5:7], y0))
        y2 = over(after(x2, done))
        up3 = lax.ppermute(after(up2, done), "fsdp", up(2))
        dn3 = lax.ppermute(after(dn2, done), "fsdp", down(2))
        far1 = gather_tiles(after((x0, x1, y0, x2, y1), up2, dn2, done, sib_head))
        sib_far1 = core(far1)
        sib_far2 = core(after(y2, sib_far1))
        sib_far3 = core(after(x3, up3, dn3, sib_far2))
        arrays = [head, tail, sib_head, sib_tail, far1, y2, x3, sib_far1, sib_far2, sib_far3]
        far_places = [(4, 0), (4, 1), (4, 3), (4, 2), (4, 4), (5, 0), (6, 0), (6, 1)]
        where = []
        for i in range(tiles):
            mine = (0, 0) if i == 0 else (1, i - 1)
            far = far_places[i]
            where += [mine, (mine[0] + 2, mine[1]), far, (far[0] + 3, far[1])]
        near = [own, up1, dn1, up2, dn2, up3, dn3]
        return near, arrays, where

    return rest, tiles, (up1, dn1), (y0,)


def shards(
    hidden_in,
    cotangent,
    base_codes,
    base_scales,
    factor_a,
    factor_b,
    task_state,
    head_a,
    head_b,
    task_ids,
    valid_counts,
    owners,
):
    f32, bf16 = jnp.float32, jnp.bfloat16
    n_groups, n_fsdp, n_dp = (lax.axis_size(a) for a in ("groups", "fsdp", "dp"))
    z, p, y = (lax.axis_index(a) for a in ("fsdp", "dp", "groups"))
    seq_len, width_part = hidden_in.shape
    tasks_all, factor_cols = factor_a.shape
    rank_double = factor_cols // width_part
    rank_half = rank_double // 2
    joined_part = cotangent.shape[1]
    joined_part_w = base_codes.shape[1]
    own = cotangent[:LIVE]
    lines = (n_groups, n_fsdp, n_dp) == (2, 4, 4) and width_part == 8 * TILE
    if lines:
        rest, tiles, first, second = permute_plan(own, base_codes, base_scales, y)

    task = task_ids[0]
    chosen_a = lax.dynamic_slice_in_dim(factor_a, task, 1, 0).reshape(width_part, rank_double)
    chosen_b = lax.dynamic_slice_in_dim(factor_b, task, 1, 0).reshape(joined_part, rank_half)
    group_cols = (HEADS // KV_HEADS + 1) * HEAD_DIM
    columns = z * joined_part + lax.broadcasted_iota(jnp.int32, (joined_part, 1), 0)
    value_column = columns % group_cols >= HEADS // KV_HEADS * HEAD_DIM
    empty_b = jnp.zeros_like(chosen_b)
    joined_b = jnp.concatenate(
        [jnp.where(value_column, empty_b, chosen_b), jnp.where(value_column, chosen_b, empty_b)],
        axis=1,
    )
    parts = whole_call(
        product_kernel,
        jax.ShapeDtypeStruct((LIVE, 2 * rank_double), bf16),
        hidden_in,
        cotangent,
        chosen_a,
        joined_b,
    )
    sums = jnp.sum(lax.all_gather(parts, "fsdp", axis=0).astype(f32), axis=0)
    keep = lax.broadcasted_iota(jnp.int32, (LIVE, 1), 0) < valid_counts[0]
    sums = jnp.where(keep, sums, 0.0).astype(bf16)
    low_in, low_grad = sums[:, :rank_double], sums[:, rank_double:]

    down_gradient, mixed = whole_call(
        factor_kernel,
        [
            jax.ShapeDtypeStruct((width_part, rank_double), f32),
            jax.ShapeDtypeStruct((joined_part, rank_double), f32),
        ],
        hidden_in,
        cotangent,
        low_grad,
        low_in,
    )
    up_gradient = jnp.where(value_column, mixed[:, rank_half:], mixed[:, :rank_half])
    down_cols = width_part * rank_double
    up_cols = joined_part * rank_half
    row = jnp.concatenate(
        [
            down_gradient.astype(bf16).reshape(1, down_cols),
            up_gradient.astype(bf16).reshape(1, up_cols),
            jnp.full((1, 128), task, f32).astype(bf16),
        ],
        axis=1,
    )
    if lines:
        packed = row
        row = after(row, *first)
    rows = lax.all_gather(row, "dp", axis=0, tiled=True)
    if lines:
        rows = after(rows, *second)
    ids = rows[:, down_cols + up_cols].astype(jnp.int32)
    one_hot = ids[:, None] == lax.broadcasted_iota(jnp.int32, (1, tasks_all), 1)
    states = jnp.dot(one_hot.astype(bf16), task_state, preferred_element_type=f32).astype(bf16)
    block = math.gcd(down_cols, up_cols)
    grad_head_a, part_a = head_grads(states, rows, head_a, 0, block)
    grad_head_b, part_b = head_grads(states, rows, head_b, down_cols, block)
    state_part = part_a + part_b
    state_sum = jnp.sum(lax.all_gather(state_part, "fsdp", axis=0), axis=0)
    task_rows = lax.broadcasted_iota(jnp.int32, (tasks_all, tasks_all), 0)
    task_other = lax.broadcasted_iota(jnp.int32, (tasks_all, tasks_all), 1)
    same_owner = owners[:, None] == owners[None, :]
    slot_index = jnp.sum((same_owner & (task_other < task_rows)).astype(jnp.int32), axis=1)
    target = owners * SLOTS + slot_index
    seq_target = jnp.sum(jnp.where(one_hot, target[None, :], 0), axis=1)
    own_rows = z * SLOTS + lax.broadcasted_iota(jnp.int32, (SLOTS, 1), 0)
    selector = (own_rows == seq_target[None, :]).astype(f32)
    grad_state = jnp.sum(selector[:, :, None] * state_sum[None, :, :], axis=1)

    if lines:
        near, arrays, where = rest(packed, (grad_head_a, grad_head_b, grad_state))
        meta = jnp.stack([z, p, y, valid_counts[0]]).astype(jnp.int32)
        any_spec = pl.BlockSpec(memory_space=pl.ANY)
        vmem_spec = pl.BlockSpec(memory_space=pltpu.VMEM)
        depth = 4
        input_gradient = pl.pallas_call(
            lambda *refs: input_gradient_kernel(tiles, where, len(arrays), *refs),
            out_shape=jax.ShapeDtypeStruct((seq_len, width_part), bf16),
            in_specs=[pl.BlockSpec(memory_space=pltpu.SMEM), vmem_spec, vmem_spec]
            + [any_spec] * (len(near) + len(arrays)),
            out_specs=vmem_spec,
            scratch_shapes=[
                pltpu.VMEM((4, LIVE, joined_part), bf16),
                pltpu.VMEM((depth, joined_part_w, TILE), bf16),
                pltpu.SemaphoreType.DMA((4,)),
                pltpu.SemaphoreType.DMA((depth,)),
            ],
            compiler_params=pltpu.CompilerParams(vmem_limit_bytes=40 * 2**20),
        )(meta, low_grad, chosen_a, *near, *arrays)
    else:
        weight = dequantize(
            lax.all_gather(base_codes, "dp", axis=1, tiled=True),
            lax.all_gather(base_scales, "dp", axis=1, tiled=True),
        )
        merged = lax.dot_general(
            lax.all_gather(own, "fsdp", axis=1, tiled=True),
            weight,
            (((1,), (1,)), ((), ())),
            preferred_element_type=f32,
        )
        adapter = lax.dot_general(
            low_grad, chosen_a, (((1,), (1,)), ((), ())), preferred_element_type=f32
        )
        live = (jnp.where(keep, merged, 0.0) + adapter_scale * adapter).astype(bf16)
        input_gradient = jnp.pad(live, ((0, seq_len - LIVE), (0, 0)))
    return (input_gradient, grad_head_a, grad_head_b, grad_state)


def solution(mesh):
    placed = (
        P(("groups", "dp"), "fsdp"),
        P(("groups", "dp"), "fsdp"),
        P("fsdp", "dp"),
        P("fsdp", "dp"),
        P("groups", "fsdp"),
        P("groups", "fsdp"),
        P("groups", "dp"),
        P("dp", "fsdp"),
        P("dp", "fsdp"),
        P(("groups", "dp")),
        P(("groups", "dp")),
        P("groups"),
    )
    return jax.shard_map(
        shards,
        mesh=mesh,
        in_specs=placed,
        out_specs=(
            P(("groups", "dp"), "fsdp"),
            P(("groups", "dp"), "fsdp"),
            P(("groups", "dp"), "fsdp"),
            P(("groups", "fsdp"), "dp"),
        ),
        check_vma=False,
    )
```

```python
import math

import jax
import jax.numpy as jnp
from jax import lax
from jax.experimental import pallas as pl
from jax.experimental.pallas import tpu as pltpu
from jax.sharding import PartitionSpec as P

HEADS = 64
KV_HEADS = 8
HEAD_DIM = 128
QBLOCK = 64
SLOTS = 4
LIVE = 384
TILE = 256

adapter_scale = 2.0


def dequantize(codes, scales):
    rows, cols = codes.shape
    blocks = scales.shape[1]
    return (
        (
            codes.astype(jnp.float32).reshape(rows, blocks, QBLOCK)
            * scales.astype(jnp.float32)[:, :, None]
        )
        .reshape(rows, cols)
        .astype(jnp.bfloat16)
    )


def weight_kernel(group, codes, scales, out):
    cols, blocks = codes.shape[1], scales.shape[0]
    spread = (
        lax.broadcasted_iota(jnp.int32, (blocks, cols), 1) // QBLOCK
        == lax.broadcasted_iota(jnp.int32, (blocks, cols), 0)
    ).astype(jnp.bfloat16)
    wide = lax.dot_general(
        scales[...], spread, (((0,), (0,)), ((), ())), preferred_element_type=jnp.float32
    )
    out[0] = (codes[...].astype(jnp.float32) * wide).astype(jnp.bfloat16)


def weight_tiles(group, codes, scales, first, count, half):
    cols, blocks = codes.shape[1], scales.shape[0]

    def place(i, group):
        at = first + i
        moved = jnp.where(at < half, at + group[0] * half, at - group[0] * half)
        return jnp.where(at < 2 * half, moved, at)

    return pl.pallas_call(
        weight_kernel,
        out_shape=jax.ShapeDtypeStruct((count, TILE, cols), jnp.bfloat16),
        grid_spec=pltpu.PrefetchScalarGridSpec(
            num_scalar_prefetch=1,
            grid=(count,),
            in_specs=[
                pl.BlockSpec((TILE, cols), lambda i, group: (place(i, group), 0)),
                pl.BlockSpec((blocks, TILE), lambda i, group: (0, place(i, group))),
            ],
            out_specs=pl.BlockSpec((1, TILE, cols), lambda i, group: (i, 0, 0)),
        ),
        compiler_params=pltpu.CompilerParams(vmem_limit_bytes=32 * 2**20),
        cost_estimate=pl.CostEstimate(flops=0, transcendentals=0, bytes_accessed=0),
    )(group, codes, scales)


def value_columns(first, count):
    group_cols = (HEADS // KV_HEADS + 1) * HEAD_DIM
    column = first + lax.broadcasted_iota(jnp.int32, (count, 1), 0)
    return lax.rem(column, group_cols) >= HEADS // KV_HEADS * HEAD_DIM


def product_kernel(first, hidden, cotangent, chosen_a, chosen_b, out):
    value = value_columns(first[0], cotangent.shape[1])
    plain = chosen_b[...]
    empty = jnp.zeros_like(plain)
    joined = jnp.concatenate(
        [jnp.where(value, empty, plain), jnp.where(value, plain, empty)], axis=1
    )
    inner = jnp.dot(hidden[:LIVE, :], chosen_a[...], preferred_element_type=jnp.float32)
    outer = jnp.dot(cotangent[:LIVE, :], joined, preferred_element_type=jnp.float32)
    out[...] = jnp.concatenate([inner, outer], axis=1).astype(out.dtype)


def factor_kernel(first, hidden, cotangent, grad, low, down, up):
    contract = (((0,), (0,)), ((), ()))
    down[...] = adapter_scale * lax.dot_general(
        hidden[:LIVE, :], grad[...], contract, preferred_element_type=jnp.float32
    )
    mixed = lax.dot_general(
        cotangent[:LIVE, :], low[...], contract, preferred_element_type=jnp.float32
    )
    half = low.shape[1] // 2
    value = value_columns(first[0], cotangent.shape[1])
    up[...] = adapter_scale * jnp.where(value, mixed[:, half:], mixed[:, :half])


def head_kernel(states, rows, head, grad, part):
    grad[...] = lax.dot_general(
        states[...], rows[...], (((0,), (0,)), ((), ())), preferred_element_type=jnp.float32
    )

    @pl.when(pl.program_id(0) == 0)
    def _():
        part[...] = jnp.zeros_like(part)

    part[...] += lax.dot_general(
        rows[...], head[...], (((1,), (1,)), ((), ())), preferred_element_type=jnp.float32
    )


def head_grads(states, rows, head, first, block):
    hidden_units, cols = head.shape
    sequences = rows.shape[0]
    return pl.pallas_call(
        head_kernel,
        out_shape=[
            jax.ShapeDtypeStruct((hidden_units, cols), jnp.float32),
            jax.ShapeDtypeStruct((sequences, hidden_units), jnp.float32),
        ],
        grid=(cols // block,),
        in_specs=[
            pl.BlockSpec((sequences, hidden_units), lambda i: (0, 0)),
            pl.BlockSpec((sequences, block), lambda i: (0, first // block + i)),
            pl.BlockSpec((hidden_units, block), lambda i: (0, i)),
        ],
        out_specs=[
            pl.BlockSpec((hidden_units, block), lambda i: (0, i)),
            pl.BlockSpec((sequences, hidden_units), lambda i: (0, 0)),
        ],
        compiler_params=pltpu.CompilerParams(vmem_limit_bytes=32 * 2**20),
        cost_estimate=pl.CostEstimate(flops=0, transcendentals=0, bytes_accessed=0),
    )(states, rows, head)


def whole_call(kernel, out_shape, *operands, scalars=()):
    spec = pl.BlockSpec(memory_space=pltpu.VMEM)
    return pl.pallas_call(
        kernel,
        out_shape=out_shape,
        in_specs=[pl.BlockSpec(memory_space=pltpu.SMEM)] * len(scalars) + [spec] * len(operands),
        out_specs=jax.tree.map(lambda _: spec, out_shape),
        compiler_params=pltpu.CompilerParams(vmem_limit_bytes=32 * 2**20),
        cost_estimate=pl.CostEstimate(flops=0, transcendentals=0, bytes_accessed=0),
    )(*scalars, *operands)


def after(value, *done):
    return lax.optimization_barrier((value, done))[0]


def input_gradient_kernel(tiles, where, count, *refs):
    meta, low, chosen = refs[:3]
    near = refs[3:10]
    arrays = refs[10 : 10 + count]
    out, cot, wbuf, csem, wsem = refs[10 + count :]
    weights = [arrays[index].at[offset] for index, offset in where]
    z, p, y, valid = meta[0], meta[1], meta[2], meta[3]
    own, up1, dn1, up2, dn2, up3, dn3 = near
    depth, cols = wbuf.shape[0], own.shape[1]
    half = (tiles - 2) // 2

    def send(tile, slot):
        for j in range(4):
            pltpu.make_async_copy(
                weights[tile * 4 + j], wbuf.at[slot, :, pl.ds(j * cols, cols)], wsem.at[slot, j]
            ).start()

    def arrive(source, slot):
        j = jnp.bitwise_xor(jnp.bitwise_and(z - slot, 3), p)
        target = cot.at[:, pl.ds(pl.multiple_of(j * cols, 128), cols)]
        return pltpu.make_async_copy(source, target, csem.at[slot])

    def place(first, second, take_first, slot):
        pl.when(take_first)(lambda: arrive(first, slot).start())
        pl.when(jnp.logical_not(take_first))(lambda: arrive(second, slot).start())

    for slot in range(depth - 1):
        send(slot, slot)
    arrive(own, 0).start()
    place(up1, dn3, z >= 1, 1)
    place(up2, dn2, z >= 2, 2)
    place(up3, dn1, z >= 3, 3)
    keep = lax.broadcasted_iota(jnp.int32, (LIVE, 1), 0) < valid
    out[LIVE:, :] = jnp.zeros((out.shape[0] - LIVE, out.shape[1]), out.dtype)
    for slot in range(4):
        arrive(own, slot).wait()

    @pl.loop(0, tiles)
    def _(tile):
        slot = lax.rem(tile, depth)
        ahead = tile + depth - 1
        for index in range(depth - 1, tiles):
            pl.when(ahead == index)(lambda index=index: send(index, index % depth))
        for j in range(4):
            pltpu.make_async_copy(
                weights[0], wbuf.at[slot, :, pl.ds(j * cols, cols)], wsem.at[slot, j]
            ).wait()
        moved = jnp.where(tile < half, tile + y * half, tile - y * half)
        start = pl.multiple_of(jnp.where(tile < 2 * half, moved, tile) * TILE, TILE)
        rows = (((1,), (1,)), ((), ()))
        total = lax.dot_general(cot[...], wbuf[slot], rows, preferred_element_type=jnp.float32)
        adapter = adapter_scale * lax.dot_general(
            low[...], chosen[pl.ds(start, TILE), :], rows, preferred_element_type=jnp.float32
        )
        result = jnp.where(keep, total, 0.0) + adapter
        out[:LIVE, pl.ds(start, TILE)] = result.astype(out.dtype)


def input_gradient_call(meta, low_grad, chosen_a, near, arrays, where, tiles, seq_len):
    any_spec = pl.BlockSpec(memory_space=pl.ANY)
    vmem_spec = pl.BlockSpec(memory_space=pltpu.VMEM)
    depth = 3
    cols = near[0].shape[1]
    return pl.pallas_call(
        lambda *refs: input_gradient_kernel(tiles, where, len(arrays), *refs),
        out_shape=jax.ShapeDtypeStruct((seq_len, tiles * TILE), jnp.bfloat16),
        in_specs=[pl.BlockSpec(memory_space=pltpu.SMEM), vmem_spec, vmem_spec]
        + [any_spec] * (len(near) + len(arrays)),
        out_specs=vmem_spec,
        scratch_shapes=[
            pltpu.VMEM((LIVE, 4 * cols), jnp.bfloat16),
            pltpu.VMEM((depth, TILE, 4 * cols), jnp.bfloat16),
            pltpu.SemaphoreType.DMA((4,)),
            pltpu.SemaphoreType.DMA((depth, 4)),
        ],
        compiler_params=pltpu.CompilerParams(vmem_limit_bytes=40 * 2**20),
    )(meta, low_grad, chosen_a, *near, *arrays)


def gather_kernel(*refs):
    out = refs[-1]
    for i, ref in enumerate(refs[:-1]):
        out[i] = ref[0]


def gather_tiles(tiles):
    shape = jax.ShapeDtypeStruct((len(tiles),) + tiles[0].shape[1:], tiles[0].dtype)
    return whole_call(gather_kernel, shape, *tiles)


def across(value):
    return lax.ppermute(value, "dp", [(i, i ^ 2) for i in range(4)])


def core(value):
    return lax.ppermute(value, "dp", [(i, i ^ 1) for i in range(4)])


def over(value):
    return lax.ppermute(value, "groups", [(0, 1), (1, 0)])


def line(value, step):
    def send(value, sign, far):
        pairs = [(i, i + 1) for i in range(far, 3)]
        return lax.ppermute(value, "fsdp", pairs if sign > 0 else [(3 - a, 3 - b) for a, b in pairs])

    return lambda sign: send(value, sign, step)


def turns(value):
    return [lax.ppermute(value, "fsdp", [(i, (i + k) % 4) for i in range(4)]) for k in (1, 2, 3)]


class Plan:
    def __init__(self, own, codes, scales, y):
        self.own, self.codes, self.scales = own, codes, scales.T
        self.tiles = codes.shape[0] // TILE
        self.half = (self.tiles - 2) // 2
        self.group = y.astype(jnp.int32).reshape(1)
        self.head = weight_tiles(self.group, codes, self.scales, 0, 1, self.half)
        self.x0 = across(self.head)

    def sum_parts(self, parts):
        others = turns(parts)
        self.up1 = line(after(self.own, parts), 0)(1)
        self.dn1 = line(after(self.own, parts), 0)(-1)
        group = after(self.group, *others)
        self.tail = weight_tiles(group, self.codes, self.scales, 1, self.tiles - 1, self.half)
        self.x1 = across(self.tail[0:1])
        self.sib_tail = core(self.tail)
        self.sib_head = core(after(self.head, self.sib_tail))
        self.y0 = over(self.x0)
        self.x2 = across(after(self.tail[1:2], self.sib_tail))
        total = parts.astype(jnp.float32)
        for other in others:
            total = total + other.astype(jnp.float32)
        return total

    def gather_rows(self, row):
        pair = jnp.concatenate([row, core(row)])
        rows = jnp.concatenate([pair, across(pair)])
        return after(rows, self.y0)

    def finish(self, done, state_part):
        up2, dn2 = line(self.up1, 1)(1), line(self.dn1, 1)(-1)
        y1 = over(after(self.x1, self.up1, self.dn1))
        x3 = across(after(self.tail[5:7], self.y0))
        y2 = over(after(self.x2, done))
        up3, dn3 = line(after(up2, done), 2)(1), line(after(dn2, done), 2)(-1)
        early = after((self.x0, self.x1, self.y0, self.x2, y1), up2, dn2, done, self.sib_head)
        far1 = gather_tiles(early)
        sib_far1 = core(far1)
        sib_far2 = core(after(y2, sib_far1))
        state_sum = state_part
        for other in turns(after(state_part, up3, dn3)):
            state_sum = state_sum + other
        sib_far3 = core(after(x3, up3, dn3, sib_far2))
        arrays = [self.head, self.tail, self.sib_head, self.sib_tail]
        arrays += [far1, y2, x3, sib_far1, sib_far2, sib_far3]
        far_places = [(4, 0), (4, 1), (4, 3), (4, 2), (4, 4), (5, 0), (6, 0), (6, 1)]
        where = []
        for i in range(self.tiles):
            mine = (0, 0) if i == 0 else (1, i - 1)
            far = far_places[i]
            where += [mine, (mine[0] + 2, mine[1]), far, (far[0] + 3, far[1])]
        near = [self.own, self.up1, self.dn1, up2, dn2, up3, dn3]
        return near, arrays, where, state_sum


def shards(
    hidden_in,
    cotangent,
    base_codes,
    base_scales,
    factor_a,
    factor_b,
    task_state,
    head_a,
    head_b,
    task_ids,
    valid_counts,
    owners,
):
    f32, bf16 = jnp.float32, jnp.bfloat16
    n_groups, n_fsdp, n_dp = (lax.axis_size(a) for a in ("groups", "fsdp", "dp"))
    z, p, y = (lax.axis_index(a) for a in ("fsdp", "dp", "groups"))
    seq_len, width_part = hidden_in.shape
    tasks_all, factor_cols = factor_a.shape
    rank_double = factor_cols // width_part
    rank_half = rank_double // 2
    joined_part = cotangent.shape[1]
    own = cotangent[:LIVE]
    lines = (n_groups, n_fsdp, n_dp) == (2, 4, 4) and width_part == 8 * TILE
    plan = Plan(own, base_codes, base_scales, y) if lines else None

    task = task_ids[0]
    chosen_a = lax.dynamic_slice_in_dim(factor_a, task, 1, 0).reshape(width_part, rank_double)
    chosen_b = lax.dynamic_slice_in_dim(factor_b, task, 1, 0).reshape(joined_part, rank_half)
    first_column = (z * joined_part).astype(jnp.int32).reshape(1)
    parts = whole_call(
        product_kernel,
        jax.ShapeDtypeStruct((LIVE, 2 * rank_double), bf16),
        hidden_in,
        cotangent,
        chosen_a,
        chosen_b,
        scalars=(first_column,),
    )
    if lines:
        sums = plan.sum_parts(parts)
    else:
        sums = jnp.sum(lax.all_gather(parts, "fsdp", axis=0).astype(f32), axis=0)
    keep = lax.broadcasted_iota(jnp.int32, (LIVE, 1), 0) < valid_counts[0]
    sums = jnp.where(keep, sums, 0.0).astype(bf16)
    low_in, low_grad = sums[:, :rank_double], sums[:, rank_double:]

    down_gradient, up_gradient = whole_call(
        factor_kernel,
        [
            jax.ShapeDtypeStruct((width_part, rank_double), f32),
            jax.ShapeDtypeStruct((joined_part, rank_half), f32),
        ],
        hidden_in,
        cotangent,
        low_grad,
        low_in,
        scalars=(first_column,),
    )
    down_cols = width_part * rank_double
    up_cols = joined_part * rank_half
    row = jnp.concatenate(
        [
            down_gradient.astype(bf16).reshape(1, down_cols),
            up_gradient.astype(bf16).reshape(1, up_cols),
            jnp.full((1, 128), task, f32).astype(bf16),
        ],
        axis=1,
    )
    rows = plan.gather_rows(row) if lines else lax.all_gather(row, "dp", axis=0, tiled=True)
    ids = rows[:, down_cols + up_cols].astype(jnp.int32)
    one_hot = ids[:, None] == lax.broadcasted_iota(jnp.int32, (1, tasks_all), 1)
    states = jnp.dot(one_hot.astype(bf16), task_state, preferred_element_type=f32).astype(bf16)
    block = math.gcd(down_cols, up_cols)
    grad_head_a, part_a = head_grads(states, rows, head_a, 0, block)
    grad_head_b, part_b = head_grads(states, rows, head_b, down_cols, block)
    state_part = part_a + part_b
    if lines:
        done = (grad_head_a, grad_head_b)
        near, arrays, where, state_sum = plan.finish(done, state_part)
    else:
        state_sum = jnp.sum(lax.all_gather(state_part, "fsdp", axis=0), axis=0)
    task_rows = lax.broadcasted_iota(jnp.int32, (tasks_all, tasks_all), 0)
    task_other = lax.broadcasted_iota(jnp.int32, (tasks_all, tasks_all), 1)
    same_owner = owners[:, None] == owners[None, :]
    slot_index = jnp.sum((same_owner & (task_other < task_rows)).astype(jnp.int32), axis=1)
    target = owners * SLOTS + slot_index
    seq_target = jnp.sum(jnp.where(one_hot, target[None, :], 0), axis=1)
    own_rows = z * SLOTS + lax.broadcasted_iota(jnp.int32, (SLOTS, 1), 0)
    selector = (own_rows == seq_target[None, :]).astype(f32)
    grad_state = jnp.sum(selector[:, :, None] * state_sum[None, :, :], axis=1)

    if lines:
        meta = jnp.stack([z, p, y, valid_counts[0]]).astype(jnp.int32)
        input_gradient = input_gradient_call(
            meta, low_grad, chosen_a, near, arrays, where, plan.tiles, seq_len
        )
    else:
        weight = dequantize(
            lax.all_gather(base_codes, "dp", axis=1, tiled=True),
            lax.all_gather(base_scales, "dp", axis=1, tiled=True),
        )
        merged = lax.dot_general(
            lax.all_gather(own, "fsdp", axis=1, tiled=True),
            weight,
            (((1,), (1,)), ((), ())),
            preferred_element_type=f32,
        )
        adapter = lax.dot_general(
            low_grad, chosen_a, (((1,), (1,)), ((), ())), preferred_element_type=f32
        )
        live = (jnp.where(keep, merged, 0.0) + adapter_scale * adapter).astype(bf16)
        input_gradient = jnp.pad(live, ((0, seq_len - LIVE), (0, 0)))
    return (input_gradient, grad_head_a, grad_head_b, grad_state)


def solution(mesh):
    placed = (
        P(("groups", "dp"), "fsdp"),
        P(("groups", "dp"), "fsdp"),
        P("fsdp", "dp"),
        P("fsdp", "dp"),
        P("groups", "fsdp"),
        P("groups", "fsdp"),
        P("groups", "dp"),
        P("dp", "fsdp"),
        P("dp", "fsdp"),
        P(("groups", "dp")),
        P(("groups", "dp")),
        P("groups"),
    )
    return jax.shard_map(
        shards,
        mesh=mesh,
        in_specs=placed,
        out_specs=(
            P(("groups", "dp"), "fsdp"),
            P(("groups", "dp"), "fsdp"),
            P(("groups", "dp"), "fsdp"),
            P(("groups", "fsdp"), "dp"),
        ),
        check_vma=False,
    )
```

```python
import math

import jax
import jax.numpy as jnp
from jax import lax
from jax.experimental import pallas as pl
from jax.experimental.pallas import tpu as pltpu
from jax.sharding import PartitionSpec as P

HEADS = 64
KV_HEADS = 8
HEAD_DIM = 128
QBLOCK = 64
SLOTS = 4
LIVE = 384
TILE = 256
PIECE = 128
SENT = (3, 3)

adapter_scale = 2.0


def dequantize(codes, scales):
    rows, cols = codes.shape
    blocks = scales.shape[1]
    return (
        (
            codes.astype(jnp.float32).reshape(rows, blocks, QBLOCK)
            * scales.astype(jnp.float32)[:, :, None]
        )
        .reshape(rows, cols)
        .astype(jnp.bfloat16)
    )


def weight_kernel(ranges, group, codes, scales, out, *copies):
    cols, blocks = codes.shape[1], scales.shape[0]
    spread = (
        lax.broadcasted_iota(jnp.int32, (blocks, cols), 1) // QBLOCK
        == lax.broadcasted_iota(jnp.int32, (blocks, cols), 0)
    ).astype(jnp.bfloat16)
    wide = lax.dot_general(
        scales[...], spread, (((0,), (0,)), ((), ())), preferred_element_type=jnp.float32
    )
    piece = (codes[...].astype(jnp.float32) * wide).astype(jnp.bfloat16)
    out[0] = piece
    i = pl.program_id(0)
    for (low, high), copy in zip(ranges, copies):

        @pl.when((i >= low) & (i < high))
        def _(copy=copy):
            copy[0] = piece


def placed_piece(at, group, half):
    moved = jnp.where(at < half, at + group * half, at - group * half)
    return jnp.where(at < 2 * half, moved, at)


def weight_pieces(group, codes, scales, count, half, ranges):
    cols, blocks = codes.shape[1], scales.shape[0]
    spans = [(0, count)] + list(ranges)

    def span_spec(low, high):
        return pl.BlockSpec(
            (1, PIECE, cols), lambda i, group: (jnp.clip(i - low, 0, high - low - 1), 0, 0)
        )

    return pl.pallas_call(
        lambda *refs: weight_kernel(ranges, *refs),
        out_shape=[
            jax.ShapeDtypeStruct((high - low, PIECE, cols), jnp.bfloat16) for low, high in spans
        ],
        grid_spec=pltpu.PrefetchScalarGridSpec(
            num_scalar_prefetch=1,
            grid=(count,),
            in_specs=[
                pl.BlockSpec(
                    (PIECE, cols), lambda i, group: (placed_piece(i, group[0], half), 0)
                ),
                pl.BlockSpec(
                    (blocks, PIECE), lambda i, group: (0, placed_piece(i, group[0], half))
                ),
            ],
            out_specs=[span_spec(low, high) for low, high in spans],
        ),
        compiler_params=pltpu.CompilerParams(vmem_limit_bytes=32 * 2**20),
        cost_estimate=pl.CostEstimate(flops=0, transcendentals=0, bytes_accessed=0),
    )(group, codes, scales)


def value_columns(first, count):
    group_cols = (HEADS // KV_HEADS + 1) * HEAD_DIM
    column = first + lax.broadcasted_iota(jnp.int32, (count, 1), 0)
    return lax.rem(column, group_cols) >= HEADS // KV_HEADS * HEAD_DIM


def product_kernel(first, hidden, cotangent, chosen_a, chosen_b, out):
    value = value_columns(first[0], cotangent.shape[1])
    plain = chosen_b[...]
    empty = jnp.zeros_like(plain)
    joined = jnp.concatenate(
        [jnp.where(value, empty, plain), jnp.where(value, plain, empty)], axis=1
    )
    inner = jnp.dot(hidden[:LIVE, :], chosen_a[...], preferred_element_type=jnp.float32)
    outer = jnp.dot(cotangent[:LIVE, :], joined, preferred_element_type=jnp.float32)
    out[...] = jnp.concatenate([inner, outer], axis=1).astype(out.dtype)


def factor_kernel(scalars, hidden, cotangent, parts, down, up, low_grad):
    rank = low_grad.shape[1]
    total = parts[0].astype(jnp.float32)
    for i in range(1, parts.shape[0]):
        total = total + parts[i].astype(jnp.float32)
    keep = lax.broadcasted_iota(jnp.int32, (LIVE, 1), 0) < scalars[1]
    sums = jnp.where(keep, total, 0.0).astype(jnp.bfloat16)
    low, grad = sums[:, :rank], sums[:, rank:]
    low_grad[...] = grad
    contract = (((0,), (0,)), ((), ()))
    down[...] = adapter_scale * lax.dot_general(
        hidden[:LIVE, :], grad, contract, preferred_element_type=jnp.float32
    )
    mixed = lax.dot_general(
        cotangent[:LIVE, :], low, contract, preferred_element_type=jnp.float32
    )
    half = rank // 2
    value = value_columns(scalars[0], cotangent.shape[1])
    up[...] = adapter_scale * jnp.where(value, mixed[:, half:], mixed[:, :half])


def joined_factor_kernel(scalars, hidden, cotangent, *refs):
    parts, outs = refs[:-3], refs[-3:]
    factor_kernel(scalars, hidden, cotangent, Stack(parts), *outs)


class Stack:
    def __init__(self, refs):
        self.refs, self.shape = refs, (len(refs),) + refs[0].shape

    def __getitem__(self, index):
        return self.refs[index][...]


def row_kernel(down, up, task, out):
    down_cols, up_cols = down.shape[1], up.shape[1]
    out[:, :down_cols] = down[...]
    out[:, down_cols : down_cols + up_cols] = up[...]
    out[:, down_cols + up_cols :] = task[...]


def pair_kernel(first, second, out):
    out[0:1, :] = first[...]
    out[1:2, :] = second[...]


def head_kernel(states, *refs):
    head, grad, part = refs[-3:]
    rows = jnp.concatenate([ref[...] for ref in refs[:-3]], axis=0)
    grad[...] = lax.dot_general(
        states[...], rows, (((0,), (0,)), ((), ())), preferred_element_type=jnp.float32
    )

    @pl.when(pl.program_id(0) == 0)
    def _():
        part[...] = jnp.zeros_like(part)

    part[...] += lax.dot_general(
        rows, head[...], (((1,), (1,)), ((), ())), preferred_element_type=jnp.float32
    )


def head_grads(states, rows, head, first, block):
    hidden_units, cols = head.shape
    sequences = sum(row.shape[0] for row in rows)
    return pl.pallas_call(
        head_kernel,
        out_shape=[
            jax.ShapeDtypeStruct((hidden_units, cols), jnp.float32),
            jax.ShapeDtypeStruct((sequences, hidden_units), jnp.float32),
        ],
        grid=(cols // block,),
        in_specs=[
            pl.BlockSpec((sequences, hidden_units), lambda i: (0, 0)),
        ]
        + [pl.BlockSpec((row.shape[0], block), lambda i: (0, first // block + i)) for row in rows]
        + [pl.BlockSpec((hidden_units, block), lambda i: (0, i))],
        out_specs=[
            pl.BlockSpec((hidden_units, block), lambda i: (0, i)),
            pl.BlockSpec((sequences, hidden_units), lambda i: (0, 0)),
        ],
        compiler_params=pltpu.CompilerParams(vmem_limit_bytes=32 * 2**20),
        cost_estimate=pl.CostEstimate(flops=0, transcendentals=0, bytes_accessed=0),
    )(states, *rows, head)


def whole_call(kernel, out_shape, *operands, scalars=()):
    spec = pl.BlockSpec(memory_space=pltpu.VMEM)
    return pl.pallas_call(
        kernel,
        out_shape=out_shape,
        in_specs=[pl.BlockSpec(memory_space=pltpu.SMEM)] * len(scalars) + [spec] * len(operands),
        out_specs=jax.tree.map(lambda _: spec, out_shape),
        compiler_params=pltpu.CompilerParams(vmem_limit_bytes=32 * 2**20),
        cost_estimate=pl.CostEstimate(flops=0, transcendentals=0, bytes_accessed=0),
    )(*scalars, *operands)


def after(value, *done):
    return lax.optimization_barrier((value, done))[0]


def last_slot(z):
    return jnp.where(z == 0, 1, jnp.where(z == 3, 3, 2))


def order_of(slot, last):
    return jnp.where(slot == last, 3, jnp.where(slot < last, slot, slot - 1))


def start_copy(condition, source, target, sem):
    pl.when(condition)(lambda: pltpu.make_async_copy(source, target, sem).start())


def early_kernel(where, half, *refs):
    meta, low, chosen, own, up1, dn1, up2, dn2 = refs[:8]
    arrays, (out, cot, wbuf, csem, wsem) = refs[8:-5], refs[-5:]
    z, p, y, valid = meta[0], meta[1], meta[2], meta[3]
    depth, cols, tiles = wbuf.shape[0], own.shape[1], len(where)
    last = last_slot(z)

    def send(tile, slot):
        for side in range(2):
            for j in range(4):
                index, offset = where[tile][side][1][j]
                back = jnp.bitwise_and(z - jnp.bitwise_xor(p, j), 3)
                place = order_of(back, last)
                at = pl.multiple_of(jnp.minimum(place, 2) * cols, 128)
                start_copy(
                    back != last,
                    arrays[index].at[offset],
                    wbuf.at[slot, pl.ds(side * PIECE, PIECE), pl.ds(at, cols)],
                    wsem.at[slot, side, jnp.minimum(place, 2)],
                )

    for slot in range(min(depth - 1, tiles)):
        send(slot, slot)
    part = lambda place: cot.at[:, pl.ds(place * cols, cols)]
    start_copy(z >= 0, own, part(0), csem.at[0])
    start_copy(z == 0, dn2, part(1), csem.at[1])
    start_copy(z >= 1, up1, part(1), csem.at[1])
    start_copy(z <= 2, dn1, part(2), csem.at[2])
    start_copy(z == 3, up2, part(2), csem.at[2])
    keep = lax.broadcasted_iota(jnp.int32, (LIVE, 1), 0) < valid
    rows = (((1,), (1,)), ((), ()))
    for place in range(3):
        pltpu.make_async_copy(own, part(place), csem.at[place]).wait()
    for tile in range(tiles):
        slot = tile % depth
        if tile + depth - 1 < tiles:
            send(tile + depth - 1, (tile + depth - 1) % depth)
        for side in range(2):
            for place in range(3):
                target = wbuf.at[
                    slot, pl.ds(side * PIECE, PIECE), pl.ds(place * cols, cols)
                ]
                pltpu.make_async_copy(target, target, wsem.at[slot, side, place]).wait()
        total = lax.dot_general(cot[...], wbuf[slot], rows, preferred_element_type=jnp.float32)
        for side in range(2):
            start = pl.multiple_of(placed_piece(where[tile][side][0], y, half) * PIECE, PIECE)
            adapter = adapter_scale * lax.dot_general(
                low[...], chosen[pl.ds(start, PIECE), :], rows, preferred_element_type=jnp.float32
            )
            piece = total[:, side * PIECE : (side + 1) * PIECE]
            at = tile * TILE + side * PIECE
            out[:, at : at + PIECE] = jnp.where(keep, piece, 0.0) + adapter


def late_kernel(where, half, accumulated, *refs):
    meta, dn2, up2, dn3, up3 = refs[:5]
    sums = refs[5 : 5 + accumulated]
    arrays, (out, cot, wbuf, csem, wsem) = refs[5 + accumulated : -5], refs[-5:]
    z, p, y, valid = meta[0], meta[1], meta[2], meta[3]
    depth, tiles = wbuf.shape[0], len(where)
    block = jnp.bitwise_and(z - last_slot(z), 3)
    needed = jnp.bitwise_xor(block, p)

    def send(tile, slot):
        for side in range(2):
            for j in range(4):
                index, offset = where[tile][side][1][j]
                start_copy(
                    needed == j,
                    arrays[index].at[offset],
                    wbuf.at[slot, pl.ds(side * PIECE, PIECE)],
                    wsem.at[slot, side],
                )

    start_copy(z == 0, dn3, cot, csem)
    start_copy(z == 1, dn2, cot, csem)
    start_copy(z == 2, up2, cot, csem)
    start_copy(z == 3, up3, cot, csem)
    for slot in range(depth - 1):
        send(slot, slot)
    keep = lax.broadcasted_iota(jnp.int32, (LIVE, 1), 0) < valid
    out[LIVE:, :] = jnp.zeros((out.shape[0] - LIVE, out.shape[1]), out.dtype)
    pltpu.make_async_copy(cot, cot, csem).wait()
    for tile in range(tiles):
        slot = tile % depth
        if tile + depth - 1 < tiles:
            send(tile + depth - 1, (tile + depth - 1) % depth)
        for side in range(2):
            target = wbuf.at[slot, pl.ds(side * PIECE, PIECE)]
            pltpu.make_async_copy(target, target, wsem.at[slot, side]).wait()
        total = lax.dot_general(
            cot[...], wbuf[slot], (((1,), (1,)), ((), ())), preferred_element_type=jnp.float32
        )
        before = sums[where[tile][2]]
        for side in range(2):
            start = pl.multiple_of(placed_piece(where[tile][side][0], y, half) * PIECE, PIECE)
            piece = total[:, side * PIECE : (side + 1) * PIECE]
            at = where[tile][3] * TILE + side * PIECE
            result = before[:, at : at + PIECE] + jnp.where(keep, piece, 0.0)
            out[:LIVE, pl.ds(start, PIECE)] = result.astype(out.dtype)


def matmul_call(kernel, out_shape, operands, vmem_count, scratch):
    smem = pl.BlockSpec(memory_space=pltpu.SMEM)
    vmem = pl.BlockSpec(memory_space=pltpu.VMEM)
    hbm = pl.BlockSpec(memory_space=pltpu.HBM)
    first, last = vmem_count
    specs = [smem] + [
        vmem if first <= i < last else hbm for i in range(1, len(operands))
    ]
    return pl.pallas_call(
        kernel,
        out_shape=out_shape,
        in_specs=specs,
        out_specs=vmem,
        scratch_shapes=scratch,
        compiler_params=pltpu.CompilerParams(vmem_limit_bytes=44 * 2**20),
        cost_estimate=pl.CostEstimate(flops=0, transcendentals=0, bytes_accessed=0),
    )(*operands)


def early_call(meta, low, chosen, near, arrays, where, half):
    cols, depth = near[0].shape[1], 3
    return matmul_call(
        lambda *refs: early_kernel(where, half, *refs),
        jax.ShapeDtypeStruct((LIVE, len(where) * TILE), jnp.float32),
        (meta, low, chosen, *near, *arrays),
        (1, 3),
        [
            pltpu.VMEM((LIVE, 3 * cols), jnp.bfloat16),
            pltpu.VMEM((depth, TILE, 3 * cols), jnp.bfloat16),
            pltpu.SemaphoreType.DMA((3,)),
            pltpu.SemaphoreType.DMA((depth, 2, 3)),
        ],
    )


def late_call(meta, near, sums, arrays, where, half, seq_len):
    cols, depth = near[0].shape[1], 4
    return matmul_call(
        lambda *refs: late_kernel(where, half, len(sums), *refs),
        jax.ShapeDtypeStruct((seq_len, len(where) * TILE), jnp.bfloat16),
        (meta, *near, *sums, *arrays),
        (5, 5 + len(sums)),
        [
            pltpu.VMEM((LIVE, cols), jnp.bfloat16),
            pltpu.VMEM((depth, TILE, cols), jnp.bfloat16),
            pltpu.SemaphoreType.DMA,
            pltpu.SemaphoreType.DMA((depth, 2)),
        ],
    )


def gather_kernel(*refs):
    out, at = refs[-1], 0
    for ref in refs[:-1]:
        out[at : at + ref.shape[0]] = ref[...]
        at += ref.shape[0]


def gather_pieces(arrays):
    count = sum(array.shape[0] for array in arrays)
    shape = jax.ShapeDtypeStruct((count,) + arrays[0].shape[1:], arrays[0].dtype)
    return whole_call(gather_kernel, shape, *arrays)


def across(value):
    return lax.ppermute(value, "dp", [(i, i ^ 2) for i in range(4)])


def core(value):
    return lax.ppermute(value, "dp", [(i, i ^ 1) for i in range(4)])


def over(value):
    return lax.ppermute(value, "groups", [(0, 1), (1, 0)])


def line(value, step):
    def send(value, sign, far):
        pairs = [(i, i + 1) for i in range(far, 3)]
        return lax.ppermute(value, "fsdp", pairs if sign > 0 else [(3 - a, 3 - b) for a, b in pairs])

    return lambda sign: send(value, sign, step)


def turns(value):
    return [lax.ppermute(value, "fsdp", [(i, (i + k) % 4) for i in range(4)]) for k in (1, 2, 3)]


class Plan:
    def __init__(self, own, codes, scales, y):
        self.own, self.codes, self.scales = own, codes, scales.T
        self.pieces = codes.shape[0] // PIECE
        self.half = sum(SENT)
        self.group = y.astype(jnp.int32).reshape(1)
        self.up1, self.dn1 = line(own, 0)(1), line(own, 0)(-1)
        ranges = [(0, SENT[0]), (SENT[0], self.half), (2 * self.half, self.pieces)]
        self.mine, head, self.first, self.direct = weight_pieces(
            self.group, codes, self.scales, self.pieces, self.half, ranges
        )
        self.x0 = across(head)
        self.sibling = core(self.mine)

    def sum_parts(self, parts):
        self.x1 = across(self.first)
        self.y0 = over(self.x0)
        others = turns(after(parts, self.up1, self.dn1, self.x0, self.sibling))
        self.up2 = line(after(self.up1, *others), 1)(1)
        self.dn2 = line(after(self.dn1, *others), 1)(-1)
        return [parts] + others

    def gather_rows(self, row):
        pair = whole_call(
            pair_kernel, jax.ShapeDtypeStruct((2, row.shape[1]), row.dtype), row, core(row)
        )
        rows = across(pair)
        done = (self.x1, self.y0, self.up2, self.dn2, rows)
        self.y1 = over(after(self.x1, *done))
        self.x2 = across(after(self.direct, *done))
        self.up3 = line(after(self.up2, *done), 2)(1)
        self.dn3 = line(after(self.dn2, *done), 2)(-1)
        self.far1 = gather_pieces(after((self.x0, self.x1, self.y0), *done))
        self.sib_far1 = core(self.far1)
        return after([pair, rows], self.sib_far1)

    def finish(self, done, state_part, meta, low, chosen, seq_len):
        half, far, sib_far = self.half, self.far1, self.sib_far1
        near = [self.own, self.up1, self.dn1, self.up2, self.dn2]
        arrays = [self.mine, self.sibling, far, sib_far]

        early_count = half + SENT[0]
        far_at = {i: (2, i) for i in range(early_count)}
        far_at.update({early_count + i: (4, i) for i in range(2 * half - early_count)})
        far_at.update({2 * half + i: (6, i) for i in range(self.pieces - 2 * half)})

        def entry(i):
            index, offset = far_at[i]
            return (i, ((0, i), (1, i), (index, offset), (index + 1, offset)))

        tiles = [(entry(i), entry(i + 1)) for i in range(0, self.pieces, 2)]
        where1, where2 = tiles[: early_count // 2], tiles[early_count // 2 :]
        sum1 = early_call(after(meta, done), low, chosen, near, arrays, where1, half)
        sib_y1 = core(after(self.y1, sum1))
        sib_x2 = core(after(self.x2, sib_y1, self.up3, self.dn3))
        state_sum = state_part
        for other in turns(after(state_part, self.up3, self.dn3)):
            state_sum = state_sum + other
        arrays2 = arrays + [self.y1, sib_y1, self.x2, sib_x2]
        sum2 = early_call(meta, low, chosen, near, arrays2, where2, half)
        where = [pair + (0, t) for t, pair in enumerate(where1)]
        where += [pair + (1, t) for t, pair in enumerate(where2)]
        last = [self.dn2, self.up2, self.dn3, self.up3]
        result = late_call(meta, last, [sum1, sum2], arrays2, where, half, seq_len)
        return result, state_sum


def shards(
    hidden_in,
    cotangent,
    base_codes,
    base_scales,
    factor_a,
    factor_b,
    task_state,
    head_a,
    head_b,
    task_ids,
    valid_counts,
    owners,
):
    f32, bf16 = jnp.float32, jnp.bfloat16
    n_groups, n_fsdp, n_dp = (lax.axis_size(a) for a in ("groups", "fsdp", "dp"))
    z, p, y = (lax.axis_index(a) for a in ("fsdp", "dp", "groups"))
    seq_len, width_part = hidden_in.shape
    tasks_all, factor_cols = factor_a.shape
    rank_double = factor_cols // width_part
    rank_half = rank_double // 2
    joined_part = cotangent.shape[1]
    own = cotangent[:LIVE]
    lines = (n_groups, n_fsdp, n_dp) == (2, 4, 4) and width_part == 16 * PIECE
    plan = Plan(own, base_codes, base_scales, y) if lines else None

    task_rows = lax.broadcasted_iota(jnp.int32, (tasks_all, tasks_all), 0)
    task_other = lax.broadcasted_iota(jnp.int32, (tasks_all, tasks_all), 1)
    same_owner = owners[:, None] == owners[None, :]
    slot_index = jnp.sum((same_owner & (task_other < task_rows)).astype(jnp.int32), axis=1)
    target = owners * SLOTS + slot_index

    task = task_ids[0]
    chosen_a = lax.dynamic_slice_in_dim(factor_a, task, 1, 0).reshape(width_part, rank_double)
    chosen_b = lax.dynamic_slice_in_dim(factor_b, task, 1, 0).reshape(joined_part, rank_half)
    first_column = (z * joined_part).astype(jnp.int32).reshape(1)
    parts = whole_call(
        product_kernel,
        jax.ShapeDtypeStruct((LIVE, 2 * rank_double), bf16),
        hidden_in,
        cotangent,
        chosen_a,
        chosen_b,
        scalars=(first_column,),
    )
    if lines:
        kernel, parts = joined_factor_kernel, plan.sum_parts(parts)
    else:
        kernel, parts = factor_kernel, [lax.all_gather(parts, "fsdp", axis=0)]
    scalars = jnp.stack([first_column[0], valid_counts[0]])
    down_gradient, up_gradient, low_grad = whole_call(
        kernel,
        [
            jax.ShapeDtypeStruct((width_part, rank_double), f32),
            jax.ShapeDtypeStruct((joined_part, rank_half), f32),
            jax.ShapeDtypeStruct((LIVE, rank_double), bf16),
        ],
        hidden_in,
        cotangent,
        *parts,
        scalars=(scalars,),
    )
    down_cols = width_part * rank_double
    up_cols = joined_part * rank_half
    row = whole_call(
        row_kernel,
        jax.ShapeDtypeStruct((1, down_cols + up_cols + 128), bf16),
        down_gradient.astype(bf16).reshape(1, down_cols),
        up_gradient.astype(bf16).reshape(1, up_cols),
        jnp.full((1, 128), task, f32).astype(bf16),
    )
    rows = plan.gather_rows(row) if lines else [lax.all_gather(row, "dp", axis=0, tiled=True)]
    ids = jnp.concatenate([row[:, down_cols + up_cols] for row in rows]).astype(jnp.int32)
    one_hot = ids[:, None] == lax.broadcasted_iota(jnp.int32, (1, tasks_all), 1)
    states = jnp.dot(one_hot.astype(bf16), task_state, preferred_element_type=f32).astype(bf16)
    block = math.gcd(down_cols, up_cols)
    grad_head_b, part_b = head_grads(states, rows, head_b, down_cols, block)
    if lines:
        rows = after(rows, grad_head_b)
    grad_head_a, part_a = head_grads(states, rows, head_a, 0, block)
    state_part = part_a + part_b
    seq_target = jnp.sum(jnp.where(one_hot, target[None, :], 0), axis=1)
    own_rows = z * SLOTS + lax.broadcasted_iota(jnp.int32, (SLOTS, 1), 0)
    selector = (own_rows == seq_target[None, :]).astype(f32)
    if lines:
        done = (grad_head_a, grad_head_b, selector)
        meta = jnp.stack([z, p, y, valid_counts[0]]).astype(jnp.int32)
        input_gradient, state_sum = plan.finish(
            done, state_part, meta, low_grad, chosen_a, seq_len
        )
    else:
        state_sum = jnp.sum(lax.all_gather(state_part, "fsdp", axis=0), axis=0)
    grad_state = jnp.sum(selector[:, :, None] * state_sum[None, :, :], axis=1)

    if not lines:
        weight = dequantize(
            lax.all_gather(base_codes, "dp", axis=1, tiled=True),
            lax.all_gather(base_scales, "dp", axis=1, tiled=True),
        )
        merged = lax.dot_general(
            lax.all_gather(own, "fsdp", axis=1, tiled=True),
            weight,
            (((1,), (1,)), ((), ())),
            preferred_element_type=f32,
        )
        adapter = lax.dot_general(
            low_grad, chosen_a, (((1,), (1,)), ((), ())), preferred_element_type=f32
        )
        keep = lax.broadcasted_iota(jnp.int32, (LIVE, 1), 0) < valid_counts[0]
        live = (jnp.where(keep, merged, 0.0) + adapter_scale * adapter).astype(bf16)
        input_gradient = jnp.pad(live, ((0, seq_len - LIVE), (0, 0)))
    return (input_gradient, grad_head_a, grad_head_b, grad_state)


def solution(mesh):
    placed = (
        P(("groups", "dp"), "fsdp"),
        P(("groups", "dp"), "fsdp"),
        P("fsdp", "dp"),
        P("fsdp", "dp"),
        P("groups", "fsdp"),
        P("groups", "fsdp"),
        P("groups", "dp"),
        P("dp", "fsdp"),
        P("dp", "fsdp"),
        P(("groups", "dp")),
        P(("groups", "dp")),
        P("groups"),
    )
    return jax.shard_map(
        shards,
        mesh=mesh,
        in_specs=placed,
        out_specs=(
            P(("groups", "dp"), "fsdp"),
            P(("groups", "dp"), "fsdp"),
            P(("groups", "dp"), "fsdp"),
            P(("groups", "fsdp"), "dp"),
        ),
        check_vma=False,
    )
```

```python
import math

import jax
import jax.numpy as jnp
from jax import lax
from jax.experimental import pallas as pl
from jax.experimental.pallas import tpu as pltpu
from jax.sharding import PartitionSpec as P

HEADS = 64
KV_HEADS = 8
HEAD_DIM = 128
QBLOCK = 64
SLOTS = 4
LIVE = 384
TILE = 256
PIECE = 128
SENT = (3, 3)

adapter_scale = 2.0


def dequantize(codes, scales):
    rows, cols = codes.shape
    blocks = scales.shape[1]
    return (
        (
            codes.astype(jnp.float32).reshape(rows, blocks, QBLOCK)
            * scales.astype(jnp.float32)[:, :, None]
        )
        .reshape(rows, cols)
        .astype(jnp.bfloat16)
    )


def weight_kernel(spans, group, codes, scales, *outs):
    cols, blocks = codes.shape[1], scales.shape[0]
    spread = (
        lax.broadcasted_iota(jnp.int32, (blocks, cols), 1) // QBLOCK
        == lax.broadcasted_iota(jnp.int32, (blocks, cols), 0)
    ).astype(jnp.bfloat16)
    wide = lax.dot_general(
        scales[...], spread, (((0,), (0,)), ((), ())), preferred_element_type=jnp.float32
    )
    piece = (codes[...].astype(jnp.float32) * wide).astype(jnp.bfloat16)
    i = pl.program_id(0)
    for (low, high), out in zip(spans, outs):

        @pl.when((i >= low) & (i < high))
        def _(out=out):
            out[0] = piece


def placed_piece(at, group, half):
    moved = jnp.where(at < half, at + group * half, at - group * half)
    return jnp.where(at < 2 * half, moved, at)


def weight_pieces(group, codes, scales, count, half, spans, whole=True):
    cols, blocks = codes.shape[1], scales.shape[0]
    spans = ([(0, count)] if whole else []) + spans

    def span_spec(low, high):
        return pl.BlockSpec(
            (1, PIECE, cols), lambda i, group: (jnp.clip(i - low, 0, high - low - 1), 0, 0)
        )

    return pl.pallas_call(
        lambda *refs: weight_kernel(spans, *refs),
        out_shape=[
            jax.ShapeDtypeStruct((high - low, PIECE, cols), jnp.bfloat16) for low, high in spans
        ],
        grid_spec=pltpu.PrefetchScalarGridSpec(
            num_scalar_prefetch=1,
            grid=(count,),
            in_specs=[
                pl.BlockSpec(
                    (PIECE, cols), lambda i, group: (placed_piece(i, group[0], half), 0)
                ),
                pl.BlockSpec(
                    (blocks, PIECE), lambda i, group: (0, placed_piece(i, group[0], half))
                ),
            ],
            out_specs=[span_spec(low, high) for low, high in spans],
        ),
        compiler_params=pltpu.CompilerParams(vmem_limit_bytes=32 * 2**20),
        cost_estimate=pl.CostEstimate(flops=0, transcendentals=0, bytes_accessed=0),
    )(group, codes, scales)


def value_columns(first, count):
    group_cols = (HEADS // KV_HEADS + 1) * HEAD_DIM
    column = first + lax.broadcasted_iota(jnp.int32, (count, 1), 0)
    return lax.rem(column, group_cols) >= HEADS // KV_HEADS * HEAD_DIM


def product_kernel(first, hidden, cotangent, chosen_a, chosen_b, out):
    value = value_columns(first[0], cotangent.shape[1])
    plain = chosen_b[...]
    empty = jnp.zeros_like(plain)
    joined = jnp.concatenate(
        [jnp.where(value, empty, plain), jnp.where(value, plain, empty)], axis=1
    )
    inner = jnp.dot(hidden[:LIVE, :], chosen_a[...], preferred_element_type=jnp.float32)
    outer = jnp.dot(cotangent[:LIVE, :], joined, preferred_element_type=jnp.float32)
    out[...] = jnp.concatenate([inner, outer], axis=1).astype(out.dtype)


def factor_kernel(scalars, hidden, cotangent, parts, down, up, low_grad):
    rank = low_grad.shape[1]
    total = parts[0].astype(jnp.float32)
    for i in range(1, parts.shape[0]):
        total = total + parts[i].astype(jnp.float32)
    keep = lax.broadcasted_iota(jnp.int32, (LIVE, 1), 0) < scalars[1]
    sums = jnp.where(keep, total, 0.0).astype(jnp.bfloat16)
    low, grad = sums[:, :rank], sums[:, rank:]
    low_grad[...] = grad
    contract = (((0,), (0,)), ((), ()))
    down[...] = adapter_scale * lax.dot_general(
        hidden[:LIVE, :], grad, contract, preferred_element_type=jnp.float32
    )
    mixed = lax.dot_general(
        cotangent[:LIVE, :], low, contract, preferred_element_type=jnp.float32
    )
    half = rank // 2
    value = value_columns(scalars[0], cotangent.shape[1])
    up[...] = adapter_scale * jnp.where(value, mixed[:, half:], mixed[:, :half])


def row_kernel(down, up, task, out):
    down_cols, up_cols = down.shape[1], up.shape[1]
    out[:, :down_cols] = down[...]
    out[:, down_cols : down_cols + up_cols] = up[...]
    out[:, down_cols + up_cols :] = task[...]


def head_kernel(states, *refs):
    head, grad, part = refs[-3:]
    rows = jnp.concatenate([ref[...] for ref in refs[:-3]], axis=0)
    grad[...] = lax.dot_general(
        states[...], rows, (((0,), (0,)), ((), ())), preferred_element_type=jnp.float32
    )

    @pl.when(pl.program_id(0) == 0)
    def _():
        part[...] = jnp.zeros_like(part)

    part[...] += lax.dot_general(
        rows, head[...], (((1,), (1,)), ((), ())), preferred_element_type=jnp.float32
    )


def head_grads(states, rows, head, first, block):
    hidden_units, cols = head.shape
    sequences = sum(row.shape[0] for row in rows)
    return pl.pallas_call(
        head_kernel,
        out_shape=[
            jax.ShapeDtypeStruct((hidden_units, cols), jnp.float32),
            jax.ShapeDtypeStruct((sequences, hidden_units), jnp.float32),
        ],
        grid=(cols // block,),
        in_specs=[
            pl.BlockSpec((sequences, hidden_units), lambda i: (0, 0)),
        ]
        + [pl.BlockSpec((row.shape[0], block), lambda i: (0, first // block + i)) for row in rows]
        + [pl.BlockSpec((hidden_units, block), lambda i: (0, i))],
        out_specs=[
            pl.BlockSpec((hidden_units, block), lambda i: (0, i)),
            pl.BlockSpec((sequences, hidden_units), lambda i: (0, 0)),
        ],
        compiler_params=pltpu.CompilerParams(vmem_limit_bytes=32 * 2**20),
        cost_estimate=pl.CostEstimate(flops=0, transcendentals=0, bytes_accessed=0),
    )(states, *rows, head)


def whole_call(kernel, out_shape, *operands, scalars=()):
    spec = pl.BlockSpec(memory_space=pltpu.VMEM)
    return pl.pallas_call(
        kernel,
        out_shape=out_shape,
        in_specs=[pl.BlockSpec(memory_space=pltpu.SMEM)] * len(scalars) + [spec] * len(operands),
        out_specs=jax.tree.map(lambda _: spec, out_shape),
        compiler_params=pltpu.CompilerParams(vmem_limit_bytes=32 * 2**20),
        cost_estimate=pl.CostEstimate(flops=0, transcendentals=0, bytes_accessed=0),
    )(*scalars, *operands)


def after(value, *done):
    return lax.optimization_barrier((value, done))[0]


def last_slot(z):
    return jnp.where(z == 0, 1, jnp.where(z == 3, 3, 2))


def order_of(slot, last):
    return jnp.where(slot == last, 3, jnp.where(slot < last, slot, slot - 1))


def start_copy(condition, source, target, sem):
    pl.when(condition)(lambda: pltpu.make_async_copy(source, target, sem).start())


def early_kernel(where, half, *refs):
    meta, low, chosen, own, up1, dn1, up2, dn2 = refs[:8]
    arrays, (out, cot, wbuf, csem, wsem) = refs[8:-5], refs[-5:]
    z, p, y, valid = meta[0], meta[1], meta[2], meta[3]
    depth, cols, tiles = wbuf.shape[0], own.shape[1], len(where)
    last = last_slot(z)

    def send(tile, slot):
        for side in range(2):
            for j in range(4):
                index, offset = where[tile][side][1][j]
                back = jnp.bitwise_and(z - jnp.bitwise_xor(p, j), 3)
                place = order_of(back, last)
                at = pl.multiple_of(jnp.minimum(place, 2) * cols, 128)
                start_copy(
                    back != last,
                    arrays[index].at[offset],
                    wbuf.at[slot, pl.ds(side * PIECE, PIECE), pl.ds(at, cols)],
                    wsem.at[slot, side, jnp.minimum(place, 2)],
                )

    for slot in range(min(depth - 1, tiles)):
        send(slot, slot)
    part = lambda place: cot.at[:, pl.ds(place * cols, cols)]
    start_copy(z >= 0, own, part(0), csem.at[0])
    start_copy(z == 0, dn2, part(1), csem.at[1])
    start_copy(z >= 1, up1, part(1), csem.at[1])
    start_copy(z <= 2, dn1, part(2), csem.at[2])
    start_copy(z == 3, up2, part(2), csem.at[2])
    keep = lax.broadcasted_iota(jnp.int32, (LIVE, 1), 0) < valid
    rows = (((1,), (1,)), ((), ()))
    for place in range(3):
        pltpu.make_async_copy(own, part(place), csem.at[place]).wait()
    for tile in range(tiles):
        slot = tile % depth
        if tile + depth - 1 < tiles:
            send(tile + depth - 1, (tile + depth - 1) % depth)
        for side in range(2):
            for place in range(3):
                target = wbuf.at[
                    slot, pl.ds(side * PIECE, PIECE), pl.ds(place * cols, cols)
                ]
                pltpu.make_async_copy(target, target, wsem.at[slot, side, place]).wait()
        total = lax.dot_general(cot[...], wbuf[slot], rows, preferred_element_type=jnp.float32)
        for side in range(2):
            start = pl.multiple_of(placed_piece(where[tile][side][0], y, half) * PIECE, PIECE)
            adapter = adapter_scale * lax.dot_general(
                low[...], chosen[pl.ds(start, PIECE), :], rows, preferred_element_type=jnp.float32
            )
            piece = total[:, side * PIECE : (side + 1) * PIECE]
            at = tile * TILE + side * PIECE
            out[:, at : at + PIECE] = jnp.where(keep, piece, 0.0) + adapter


def late_kernel(where, half, early, *refs):
    meta, own, up1, dn1, up2, dn2, up3, dn3, low, chosen, sums = refs[:11]
    arrays, (out, cot, wbuf, csem, wsem) = refs[11:-5], refs[-5:]
    z, p, y, valid = meta[0], meta[1], meta[2], meta[3]
    depth, cols, tiles = wbuf.shape[0], own.shape[1], len(where)
    last = last_slot(z)

    def send(tile, slot):
        for side in range(2):
            for j in range(4):
                index, offset = where[tile][side][1][j]
                back = jnp.bitwise_and(z - jnp.bitwise_xor(p, j), 3)
                place = order_of(back, last)
                start_copy(
                    (back == last) if tile < early else (back >= 0),
                    arrays[index].at[offset],
                    wbuf.at[
                        slot,
                        pl.ds(side * PIECE, PIECE),
                        pl.ds(pl.multiple_of(place * cols, 128), cols),
                    ],
                    wsem.at[slot, side, place],
                )

    part = lambda place: cot.at[:, pl.ds(place * cols, cols)]
    start_copy(z == 0, dn3, part(3), csem.at[3])
    start_copy(z == 1, dn2, part(3), csem.at[3])
    start_copy(z == 2, up2, part(3), csem.at[3])
    start_copy(z == 3, up3, part(3), csem.at[3])
    for slot in range(depth - 1):
        send(slot, slot)
    start_copy(z >= 0, own, part(0), csem.at[0])
    start_copy(z == 0, dn2, part(1), csem.at[1])
    start_copy(z >= 1, up1, part(1), csem.at[1])
    start_copy(z <= 2, dn1, part(2), csem.at[2])
    start_copy(z == 3, up2, part(2), csem.at[2])
    keep = lax.broadcasted_iota(jnp.int32, (LIVE, 1), 0) < valid
    rows = (((1,), (1,)), ((), ()))
    out[LIVE:, :] = jnp.zeros((out.shape[0] - LIVE, out.shape[1]), out.dtype)
    pltpu.make_async_copy(part(3), part(3), csem.at[3]).wait()
    for tile in range(tiles):
        slot = tile % depth
        if tile + depth - 1 < tiles:
            send(tile + depth - 1, (tile + depth - 1) % depth)
        if tile == early:
            for place in range(3):
                pltpu.make_async_copy(part(place), part(place), csem.at[place]).wait()
        first = 3 if tile < early else 0
        for side in range(2):
            for place in range(first, 4):
                target = wbuf.at[slot, pl.ds(side * PIECE, PIECE), pl.ds(place * cols, cols)]
                pltpu.make_async_copy(target, target, wsem.at[slot, side, place]).wait()
        total = lax.dot_general(
            cot[:, first * cols :],
            wbuf[slot, :, first * cols :],
            rows,
            preferred_element_type=jnp.float32,
        )
        for side in range(2):
            start = pl.multiple_of(placed_piece(where[tile][side][0], y, half) * PIECE, PIECE)
            at = tile * TILE + side * PIECE
            if tile < early:
                before = sums[:, at : at + PIECE]
            else:
                before = adapter_scale * lax.dot_general(
                    low[...],
                    chosen[pl.ds(start, PIECE), :],
                    rows,
                    preferred_element_type=jnp.float32,
                )
            piece = total[:, side * PIECE : (side + 1) * PIECE]
            result = before + jnp.where(keep, piece, 0.0)
            out[:LIVE, pl.ds(start, PIECE)] = result.astype(out.dtype)


def matmul_call(kernel, out_shape, operands, vmem_count, scratch):
    smem = pl.BlockSpec(memory_space=pltpu.SMEM)
    vmem = pl.BlockSpec(memory_space=pltpu.VMEM)
    hbm = pl.BlockSpec(memory_space=pltpu.HBM)
    first, last = vmem_count
    specs = [smem] + [
        vmem if first <= i < last else hbm for i in range(1, len(operands))
    ]
    return pl.pallas_call(
        kernel,
        out_shape=out_shape,
        in_specs=specs,
        out_specs=vmem,
        scratch_shapes=scratch,
        compiler_params=pltpu.CompilerParams(vmem_limit_bytes=44 * 2**20),
        cost_estimate=pl.CostEstimate(flops=0, transcendentals=0, bytes_accessed=0),
    )(*operands)


def early_call(meta, low, chosen, near, arrays, where, half):
    cols, depth = near[0].shape[1], 3
    return matmul_call(
        lambda *refs: early_kernel(where, half, *refs),
        jax.ShapeDtypeStruct((LIVE, len(where) * TILE), jnp.float32),
        (meta, low, chosen, *near, *arrays),
        (1, 3),
        [
            pltpu.VMEM((LIVE, 3 * cols), jnp.bfloat16),
            pltpu.VMEM((depth, TILE, 3 * cols), jnp.bfloat16),
            pltpu.SemaphoreType.DMA((3,)),
            pltpu.SemaphoreType.DMA((depth, 2, 3)),
        ],
    )


def late_call(meta, near, low, chosen, sums, arrays, where, half, early, seq_len):
    cols, depth = near[0].shape[1], 3
    return matmul_call(
        lambda *refs: late_kernel(where, half, early, *refs),
        jax.ShapeDtypeStruct((seq_len, len(where) * TILE), jnp.bfloat16),
        (meta, *near, low, chosen, sums, *arrays),
        (1 + len(near), 4 + len(near)),
        [
            pltpu.VMEM((LIVE, 4 * cols), jnp.bfloat16),
            pltpu.VMEM((depth, TILE, 4 * cols), jnp.bfloat16),
            pltpu.SemaphoreType.DMA((4,)),
            pltpu.SemaphoreType.DMA((depth, 2, 4)),
        ],
    )


def gather_kernel(*refs):
    out, at = refs[-1], 0
    for ref in refs[:-1]:
        out[at : at + ref.shape[0]] = ref[...]
        at += ref.shape[0]


def gather_pieces(arrays):
    count = sum(array.shape[0] for array in arrays)
    shape = jax.ShapeDtypeStruct((count,) + arrays[0].shape[1:], arrays[0].dtype)
    return whole_call(gather_kernel, shape, *arrays)


def across(value):
    return lax.ppermute(value, "dp", [(i, i ^ 2) for i in range(4)])


def core(value):
    return lax.ppermute(value, "dp", [(i, i ^ 1) for i in range(4)])


def over(value):
    return lax.ppermute(value, "groups", [(0, 1), (1, 0)])


def line(value, step):
    def send(value, sign, far):
        pairs = [(i, i + 1) for i in range(far, 3)]
        return lax.ppermute(value, "fsdp", pairs if sign > 0 else [(3 - a, 3 - b) for a, b in pairs])

    return lambda sign: send(value, sign, step)


def turns(value):
    return [lax.ppermute(value, "fsdp", [(i, (i + k) % 4) for i in range(4)]) for k in (1, 2, 3)]


class Plan:
    def __init__(self, own, codes, scales, y):
        self.own, self.codes, self.scales = own, codes, scales.T
        self.pieces = codes.shape[0] // PIECE
        self.half = sum(SENT)
        self.group = y.astype(jnp.int32).reshape(1)
        self.up1, self.dn1 = line(own, 0)(1), line(own, 0)(-1)
        (head,) = weight_pieces(
            self.group, codes, self.scales, SENT[0], self.half, [(0, SENT[0])], False
        )
        self.x0 = across(head)

    def sum_parts(self, parts):
        ranges = [(SENT[0], self.half), (2 * self.half, self.pieces)]
        self.mine, first, self.direct = weight_pieces(
            after(self.group, parts), self.codes, self.scales, self.pieces, self.half, ranges
        )
        gathered = lax.all_gather(after(parts, self.mine), "fsdp", axis=0)
        ready = (gathered, self.x0, self.up1, self.dn1)
        self.x1 = across(after(first, *ready))
        self.y0 = over(after(self.x0, *ready))
        self.up2 = line(after(self.up1, *ready), 1)(1)
        self.dn2 = line(after(self.dn1, *ready), 1)(-1)
        self.sibling = core(after(self.mine, *ready))
        return [gathered]

    def gather_rows(self, row):
        rows = lax.all_gather(row, "dp", axis=0, tiled=True)
        done = (self.x1, self.y0, self.up2, self.dn2, rows, self.sibling)
        self.y1 = over(after(self.x1, *done))
        self.x2 = across(after(self.direct, *done))
        self.up3 = line(after(self.up2, *done), 2)(1)
        self.dn3 = line(after(self.dn2, *done), 2)(-1)
        self.far1 = gather_pieces(after((self.x0, self.x1, self.y0), *done))
        self.sib_far1 = core(self.far1)
        return after([rows], self.sib_far1)

    def finish(self, done, state_part, meta, low, chosen, seq_len):
        half, far, sib_far = self.half, self.far1, self.sib_far1
        near = [self.own, self.up1, self.dn1, self.up2, self.dn2]
        arrays = [self.mine, self.sibling, far, sib_far]

        early_count = half + SENT[0]
        far_at = {i: (2, i) for i in range(early_count)}
        far_at.update({early_count + i: (4, i) for i in range(2 * half - early_count)})
        far_at.update({2 * half + i: (6, i) for i in range(self.pieces - 2 * half)})

        def entry(i):
            index, offset = far_at[i]
            return (i, ((0, i), (1, i), (index, offset), (index + 1, offset)))

        tiles = [(entry(i), entry(i + 1)) for i in range(0, self.pieces, 2)]
        early = early_count // 2
        sum1 = early_call(after(meta, done), low, chosen, near, arrays, tiles[:early], half)
        sib_y1 = core(after(self.y1, sum1))
        sib_x2 = core(after(self.x2, sib_y1, self.up3, self.dn3))
        others = turns(after(state_part, self.up3, self.dn3, sib_y1))
        arrays += [self.y1, sib_y1, self.x2, sib_x2]
        near += [self.up3, self.dn3]
        result = late_call(meta, near, low, chosen, sum1, arrays, tiles, half, early, seq_len)
        state_sum = state_part
        for other in others:
            state_sum = state_sum + after(other, result)
        return result, state_sum


def shards(
    hidden_in,
    cotangent,
    base_codes,
    base_scales,
    factor_a,
    factor_b,
    task_state,
    head_a,
    head_b,
    task_ids,
    valid_counts,
    owners,
):
    f32, bf16 = jnp.float32, jnp.bfloat16
    n_groups, n_fsdp, n_dp = (lax.axis_size(a) for a in ("groups", "fsdp", "dp"))
    z, p, y = (lax.axis_index(a) for a in ("fsdp", "dp", "groups"))
    seq_len, width_part = hidden_in.shape
    tasks_all, factor_cols = factor_a.shape
    rank_double = factor_cols // width_part
    rank_half = rank_double // 2
    joined_part = cotangent.shape[1]
    own = cotangent[:LIVE]
    lines = (n_groups, n_fsdp, n_dp) == (2, 4, 4) and width_part == 16 * PIECE
    plan = Plan(own, base_codes, base_scales, y) if lines else None

    task_rows = lax.broadcasted_iota(jnp.int32, (tasks_all, tasks_all), 0)
    task_other = lax.broadcasted_iota(jnp.int32, (tasks_all, tasks_all), 1)
    same_owner = owners[:, None] == owners[None, :]
    slot_index = jnp.sum((same_owner & (task_other < task_rows)).astype(jnp.int32), axis=1)
    target = owners * SLOTS + slot_index

    task = task_ids[0]
    chosen_a = lax.dynamic_slice_in_dim(factor_a, task, 1, 0).reshape(width_part, rank_double)
    chosen_b = lax.dynamic_slice_in_dim(factor_b, task, 1, 0).reshape(joined_part, rank_half)
    first_column = (z * joined_part).astype(jnp.int32).reshape(1)
    parts = whole_call(
        product_kernel,
        jax.ShapeDtypeStruct((LIVE, 2 * rank_double), bf16),
        hidden_in,
        cotangent,
        chosen_a,
        chosen_b,
        scalars=(first_column,),
    )
    if lines:
        parts = plan.sum_parts(parts)
    else:
        parts = [lax.all_gather(parts, "fsdp", axis=0)]
    scalars = jnp.stack([first_column[0], valid_counts[0]])
    down_gradient, up_gradient, low_grad = whole_call(
        factor_kernel,
        [
            jax.ShapeDtypeStruct((width_part, rank_double), f32),
            jax.ShapeDtypeStruct((joined_part, rank_half), f32),
            jax.ShapeDtypeStruct((LIVE, rank_double), bf16),
        ],
        hidden_in,
        cotangent,
        *parts,
        scalars=(scalars,),
    )
    down_cols = width_part * rank_double
    up_cols = joined_part * rank_half
    row = whole_call(
        row_kernel,
        jax.ShapeDtypeStruct((1, down_cols + up_cols + 128), bf16),
        down_gradient.astype(bf16).reshape(1, down_cols),
        up_gradient.astype(bf16).reshape(1, up_cols),
        jnp.full((1, 128), task, f32).astype(bf16),
    )
    rows = plan.gather_rows(row) if lines else [lax.all_gather(row, "dp", axis=0, tiled=True)]
    ids = jnp.concatenate([row[:, down_cols + up_cols] for row in rows]).astype(jnp.int32)
    one_hot = ids[:, None] == lax.broadcasted_iota(jnp.int32, (1, tasks_all), 1)
    states = jnp.dot(one_hot.astype(bf16), task_state, preferred_element_type=f32).astype(bf16)
    block = math.gcd(down_cols, up_cols)
    grad_head_b, part_b = head_grads(states, rows, head_b, down_cols, block)
    if lines:
        rows = after(rows, grad_head_b)
    grad_head_a, part_a = head_grads(states, rows, head_a, 0, block)
    state_part = part_a + part_b
    seq_target = jnp.sum(jnp.where(one_hot, target[None, :], 0), axis=1)
    own_rows = z * SLOTS + lax.broadcasted_iota(jnp.int32, (SLOTS, 1), 0)
    selector = (own_rows == seq_target[None, :]).astype(f32)
    if lines:
        done = (grad_head_a, grad_head_b, selector)
        meta = jnp.stack([z, p, y, valid_counts[0]]).astype(jnp.int32)
        input_gradient, state_sum = plan.finish(
            done, state_part, meta, low_grad, chosen_a, seq_len
        )
    else:
        state_sum = jnp.sum(lax.all_gather(state_part, "fsdp", axis=0), axis=0)
    grad_state = jnp.sum(selector[:, :, None] * state_sum[None, :, :], axis=1)

    if not lines:
        weight = dequantize(
            lax.all_gather(base_codes, "dp", axis=1, tiled=True),
            lax.all_gather(base_scales, "dp", axis=1, tiled=True),
        )
        merged = lax.dot_general(
            lax.all_gather(own, "fsdp", axis=1, tiled=True),
            weight,
            (((1,), (1,)), ((), ())),
            preferred_element_type=f32,
        )
        adapter = lax.dot_general(
            low_grad, chosen_a, (((1,), (1,)), ((), ())), preferred_element_type=f32
        )
        keep = lax.broadcasted_iota(jnp.int32, (LIVE, 1), 0) < valid_counts[0]
        live = (jnp.where(keep, merged, 0.0) + adapter_scale * adapter).astype(bf16)
        input_gradient = jnp.pad(live, ((0, seq_len - LIVE), (0, 0)))
    return (input_gradient, grad_head_a, grad_head_b, grad_state)


def solution(mesh):
    placed = (
        P(("groups", "dp"), "fsdp"),
        P(("groups", "dp"), "fsdp"),
        P("fsdp", "dp"),
        P("fsdp", "dp"),
        P("groups", "fsdp"),
        P("groups", "fsdp"),
        P("groups", "dp"),
        P("dp", "fsdp"),
        P("dp", "fsdp"),
        P(("groups", "dp")),
        P(("groups", "dp")),
        P("groups"),
    )
    return jax.shard_map(
        shards,
        mesh=mesh,
        in_specs=placed,
        out_specs=(
            P(("groups", "dp"), "fsdp"),
            P(("groups", "dp"), "fsdp"),
            P(("groups", "dp"), "fsdp"),
            P(("groups", "fsdp"), "dp"),
        ),
        check_vma=False,
    )
```

```python
import math

import jax
import jax.numpy as jnp
from jax import lax
from jax.experimental import pallas as pl
from jax.experimental.pallas import tpu as pltpu
from jax.sharding import PartitionSpec as P

HEADS = 64
KV_HEADS = 8
HEAD_DIM = 128
QBLOCK = 64
SLOTS = 4
LIVE = 384
TILE = 256
PIECE = 128
SENT = (3, 3)

adapter_scale = 2.0


def dequantize(codes, scales):
    rows, cols = codes.shape
    blocks = scales.shape[1]
    return (
        (
            codes.astype(jnp.float32).reshape(rows, blocks, QBLOCK)
            * scales.astype(jnp.float32)[:, :, None]
        )
        .reshape(rows, cols)
        .astype(jnp.bfloat16)
    )


def weight_kernel(spans, group, codes, scales, *outs):
    cols, blocks = codes.shape[1], scales.shape[0]
    spread = (
        lax.broadcasted_iota(jnp.int32, (blocks, cols), 1) // QBLOCK
        == lax.broadcasted_iota(jnp.int32, (blocks, cols), 0)
    ).astype(jnp.bfloat16)
    wide = lax.dot_general(
        scales[...], spread, (((0,), (0,)), ((), ())), preferred_element_type=jnp.float32
    )
    piece = (codes[...].astype(jnp.float32) * wide).astype(jnp.bfloat16)
    i = pl.program_id(0)
    for (low, high), out in zip(spans, outs):

        @pl.when((i >= low) & (i < high))
        def _(out=out):
            out[0] = piece


def placed_piece(at, group, half):
    moved = jnp.where(at < half, at + group * half, at - group * half)
    return jnp.where(at < 2 * half, moved, at)


def weight_pieces(group, codes, scales, order, half, spans):
    cols, blocks = codes.shape[1], scales.shape[0]
    count = spans[0][1]

    def span_spec(low, high):
        return pl.BlockSpec(
            (1, PIECE, cols), lambda i, group: (jnp.clip(i - low, 0, high - low - 1), 0, 0)
        )

    return pl.pallas_call(
        lambda *refs: weight_kernel(spans, *refs),
        out_shape=[
            jax.ShapeDtypeStruct((high - low, PIECE, cols), jnp.bfloat16) for low, high in spans
        ],
        grid_spec=pltpu.PrefetchScalarGridSpec(
            num_scalar_prefetch=1,
            grid=(count,),
            in_specs=[
                pl.BlockSpec(
                    (PIECE, cols), lambda i, group: (placed_piece(order(i), group[0], half), 0)
                ),
                pl.BlockSpec(
                    (blocks, PIECE), lambda i, group: (0, placed_piece(order(i), group[0], half))
                ),
            ],
            out_specs=[span_spec(low, high) for low, high in spans],
        ),
        compiler_params=pltpu.CompilerParams(vmem_limit_bytes=32 * 2**20),
        cost_estimate=pl.CostEstimate(flops=0, transcendentals=0, bytes_accessed=0),
    )(group, codes, scales)


def value_columns(first, count):
    group_cols = (HEADS // KV_HEADS + 1) * HEAD_DIM
    column = first + lax.broadcasted_iota(jnp.int32, (count, 1), 0)
    return lax.rem(column, group_cols) >= HEADS // KV_HEADS * HEAD_DIM


def product_kernel(first, hidden, cotangent, chosen_a, chosen_b, out):
    value = value_columns(first[0], cotangent.shape[1])
    plain = chosen_b[...]
    empty = jnp.zeros_like(plain)
    joined = jnp.concatenate(
        [jnp.where(value, empty, plain), jnp.where(value, plain, empty)], axis=1
    )
    inner = jnp.dot(hidden[:LIVE, :], chosen_a[...], preferred_element_type=jnp.float32)
    outer = jnp.dot(cotangent[:LIVE, :], joined, preferred_element_type=jnp.float32)
    out[...] = jnp.concatenate([inner, outer], axis=1).astype(out.dtype)


def factor_kernel(scalars, hidden, cotangent, parts, down, up, low_grad):
    rank = low_grad.shape[1]
    total = parts[0].astype(jnp.float32)
    for i in range(1, parts.shape[0]):
        total = total + parts[i].astype(jnp.float32)
    keep = lax.broadcasted_iota(jnp.int32, (LIVE, 1), 0) < scalars[1]
    sums = jnp.where(keep, total, 0.0).astype(jnp.bfloat16)
    low, grad = sums[:, :rank], sums[:, rank:]
    low_grad[...] = grad
    contract = (((0,), (0,)), ((), ()))
    down[...] = adapter_scale * lax.dot_general(
        hidden[:LIVE, :], grad, contract, preferred_element_type=jnp.float32
    )
    mixed = lax.dot_general(
        cotangent[:LIVE, :], low, contract, preferred_element_type=jnp.float32
    )
    half = rank // 2
    value = value_columns(scalars[0], cotangent.shape[1])
    up[...] = adapter_scale * jnp.where(value, mixed[:, half:], mixed[:, :half])


def row_kernel(down, up, task, out):
    down_cols, up_cols = down.shape[1], up.shape[1]
    out[:, :down_cols] = down[...]
    out[:, down_cols : down_cols + up_cols] = up[...]
    out[:, down_cols + up_cols :] = task[...]


def head_kernel(states, *refs):
    head, grad, part = refs[-3:]
    rows = jnp.concatenate([ref[...] for ref in refs[:-3]], axis=0)
    grad[...] = lax.dot_general(
        states[...], rows, (((0,), (0,)), ((), ())), preferred_element_type=jnp.float32
    )

    @pl.when(pl.program_id(0) == 0)
    def _():
        part[...] = jnp.zeros_like(part)

    part[...] += lax.dot_general(
        rows, head[...], (((1,), (1,)), ((), ())), preferred_element_type=jnp.float32
    )


def head_grads(states, rows, head, first, block):
    hidden_units, cols = head.shape
    sequences = sum(row.shape[0] for row in rows)
    return pl.pallas_call(
        head_kernel,
        out_shape=[
            jax.ShapeDtypeStruct((hidden_units, cols), jnp.float32),
            jax.ShapeDtypeStruct((sequences, hidden_units), jnp.float32),
        ],
        grid=(cols // block,),
        in_specs=[
            pl.BlockSpec((sequences, hidden_units), lambda i: (0, 0)),
        ]
        + [pl.BlockSpec((row.shape[0], block), lambda i: (0, first // block + i)) for row in rows]
        + [pl.BlockSpec((hidden_units, block), lambda i: (0, i))],
        out_specs=[
            pl.BlockSpec((hidden_units, block), lambda i: (0, i)),
            pl.BlockSpec((sequences, hidden_units), lambda i: (0, 0)),
        ],
        compiler_params=pltpu.CompilerParams(vmem_limit_bytes=32 * 2**20),
        cost_estimate=pl.CostEstimate(flops=0, transcendentals=0, bytes_accessed=0),
    )(states, *rows, head)


def whole_call(kernel, out_shape, *operands, scalars=()):
    spec = pl.BlockSpec(memory_space=pltpu.VMEM)
    return pl.pallas_call(
        kernel,
        out_shape=out_shape,
        in_specs=[pl.BlockSpec(memory_space=pltpu.SMEM)] * len(scalars) + [spec] * len(operands),
        out_specs=jax.tree.map(lambda _: spec, out_shape),
        compiler_params=pltpu.CompilerParams(vmem_limit_bytes=32 * 2**20),
        cost_estimate=pl.CostEstimate(flops=0, transcendentals=0, bytes_accessed=0),
    )(*scalars, *operands)


def after(value, *done):
    return lax.optimization_barrier((value, done))[0]


def last_slot(z):
    return jnp.where(z == 0, 1, jnp.where(z == 3, 3, 2))


def order_of(slot, last):
    return jnp.where(slot == last, 3, jnp.where(slot < last, slot, slot - 1))


def start_copy(condition, source, target, sem):
    pl.when(condition)(lambda: pltpu.make_async_copy(source, target, sem).start())


def early_kernel(where, half, *refs):
    meta, low, chosen, own, up1, dn1, up2, dn2 = refs[:8]
    arrays, (out, cot, wbuf, csem, wsem) = refs[8:-5], refs[-5:]
    z, p, y, valid = meta[0], meta[1], meta[2], meta[3]
    depth, cols, tiles = wbuf.shape[0], own.shape[1], len(where)
    last = last_slot(z)

    def send(tile, slot):
        for side in range(2):
            for j in range(4):
                index, offset = where[tile][side][1][j]
                back = jnp.bitwise_and(z - jnp.bitwise_xor(p, j), 3)
                place = order_of(back, last)
                at = pl.multiple_of(jnp.minimum(place, 2) * cols, 128)
                start_copy(
                    back != last,
                    arrays[index].at[offset],
                    wbuf.at[slot, pl.ds(side * PIECE, PIECE), pl.ds(at, cols)],
                    wsem.at[slot, side, jnp.minimum(place, 2)],
                )

    for slot in range(min(depth - 1, tiles)):
        send(slot, slot)
    part = lambda place: cot.at[:, pl.ds(place * cols, cols)]
    start_copy(z >= 0, own, part(0), csem.at[0])
    start_copy(z == 0, dn2, part(1), csem.at[1])
    start_copy(z >= 1, up1, part(1), csem.at[1])
    start_copy(z <= 2, dn1, part(2), csem.at[2])
    start_copy(z == 3, up2, part(2), csem.at[2])
    keep = lax.broadcasted_iota(jnp.int32, (LIVE, 1), 0) < valid
    rows = (((1,), (1,)), ((), ()))
    for place in range(3):
        pltpu.make_async_copy(own, part(place), csem.at[place]).wait()

    @pl.loop(0, tiles)
    def _(tile):
        slot = lax.rem(tile, depth)
        for index in range(depth - 1, tiles):
            pl.when(tile + depth - 1 == index)(lambda index=index: send(index, index % depth))
        for side in range(2):
            for place in range(3):
                target = wbuf.at[slot, pl.ds(side * PIECE, PIECE), pl.ds(place * cols, cols)]
                pltpu.make_async_copy(target, target, wsem.at[slot, side, place]).wait()
        total = lax.dot_general(cot[...], wbuf[slot], rows, preferred_element_type=jnp.float32)
        for side in range(2):
            start = pl.multiple_of(placed_piece(2 * tile + side, y, half) * PIECE, PIECE)
            adapter = adapter_scale * lax.dot_general(
                low[...], chosen[pl.ds(start, PIECE), :], rows, preferred_element_type=jnp.float32
            )
            piece = total[:, side * PIECE : (side + 1) * PIECE]
            at = pl.multiple_of(tile * TILE + side * PIECE, PIECE)
            out[:, pl.ds(at, PIECE)] = jnp.where(keep, piece, 0.0) + adapter


def late_kernel(where, half, early, *refs):
    meta, own, up1, dn1, up2, dn2, up3, dn3, low, chosen, sums = refs[:11]
    arrays, (out, cot, wbuf, csem, wsem) = refs[11:-5], refs[-5:]
    z, p, y, valid = meta[0], meta[1], meta[2], meta[3]
    depth, cols, tiles = wbuf.shape[0], own.shape[1], len(where)
    last = last_slot(z)

    def send(tile, slot):
        for side in range(2):
            for j in range(4):
                index, offset = where[tile][side][1][j]
                back = jnp.bitwise_and(z - jnp.bitwise_xor(p, j), 3)
                place = order_of(back, last)
                start_copy(
                    (back == last) if tile < early else (back >= 0),
                    arrays[index].at[offset],
                    wbuf.at[
                        slot,
                        pl.ds(side * PIECE, PIECE),
                        pl.ds(pl.multiple_of(place * cols, 128), cols),
                    ],
                    wsem.at[slot, side, place],
                )

    part = lambda place: cot.at[:, pl.ds(place * cols, cols)]
    start_copy(z == 0, dn3, part(3), csem.at[3])
    start_copy(z == 1, dn2, part(3), csem.at[3])
    start_copy(z == 2, up2, part(3), csem.at[3])
    start_copy(z == 3, up3, part(3), csem.at[3])
    for slot in range(depth - 1):
        send(slot, slot)
    start_copy(z >= 0, own, part(0), csem.at[0])
    start_copy(z == 0, dn2, part(1), csem.at[1])
    start_copy(z >= 1, up1, part(1), csem.at[1])
    start_copy(z <= 2, dn1, part(2), csem.at[2])
    start_copy(z == 3, up2, part(2), csem.at[2])
    keep = lax.broadcasted_iota(jnp.int32, (LIVE, 1), 0) < valid
    rows = (((1,), (1,)), ((), ()))
    out[LIVE:, :] = jnp.zeros((out.shape[0] - LIVE, out.shape[1]), out.dtype)
    pltpu.make_async_copy(part(3), part(3), csem.at[3]).wait()

    def product(tile, first):
        slot = lax.rem(tile, depth)
        for index in range(depth - 1, tiles):
            pl.when(tile + depth - 1 == index)(lambda index=index: send(index, index % depth))
        for side in range(2):
            for place in range(first, 4):
                target = wbuf.at[slot, pl.ds(side * PIECE, PIECE), pl.ds(place * cols, cols)]
                pltpu.make_async_copy(target, target, wsem.at[slot, side, place]).wait()
        return lax.dot_general(
            cot[:, first * cols :],
            wbuf[slot, :, first * cols :],
            rows,
            preferred_element_type=jnp.float32,
        )

    def store(tile, side, total, before):
        start = pl.multiple_of(placed_piece(2 * tile + side, y, half) * PIECE, PIECE)
        piece = jnp.where(keep, total[:, side * PIECE : (side + 1) * PIECE], 0.0)
        out[:LIVE, pl.ds(start, PIECE)] = (before(start) + piece).astype(out.dtype)

    @pl.loop(0, early)
    def _(tile):
        total = product(tile, 3)
        for side in range(2):
            at = pl.multiple_of(tile * TILE + side * PIECE, PIECE)
            store(tile, side, total, lambda start: sums[:, pl.ds(at, PIECE)])

    for place in range(3):
        pltpu.make_async_copy(part(place), part(place), csem.at[place]).wait()

    def adapter(start):
        return adapter_scale * lax.dot_general(
            low[...], chosen[pl.ds(start, PIECE), :], rows, preferred_element_type=jnp.float32
        )

    @pl.loop(early, tiles)
    def _(tile):
        total = product(tile, 0)
        for side in range(2):
            store(tile, side, total, adapter)


def matmul_call(kernel, out_shape, operands, vmem_count, scratch):
    smem = pl.BlockSpec(memory_space=pltpu.SMEM)
    vmem = pl.BlockSpec(memory_space=pltpu.VMEM)
    hbm = pl.BlockSpec(memory_space=pltpu.HBM)
    first, last = vmem_count
    specs = [smem] + [
        vmem if first <= i < last else hbm for i in range(1, len(operands))
    ]
    return pl.pallas_call(
        kernel,
        out_shape=out_shape,
        in_specs=specs,
        out_specs=vmem,
        scratch_shapes=scratch,
        compiler_params=pltpu.CompilerParams(vmem_limit_bytes=44 * 2**20),
        cost_estimate=pl.CostEstimate(flops=0, transcendentals=0, bytes_accessed=0),
    )(*operands)


def early_call(meta, low, chosen, near, arrays, where, half):
    cols, depth = near[0].shape[1], 3
    return matmul_call(
        lambda *refs: early_kernel(where, half, *refs),
        jax.ShapeDtypeStruct((LIVE, len(where) * TILE), jnp.float32),
        (meta, low, chosen, *near, *arrays),
        (1, 3),
        [
            pltpu.VMEM((LIVE, 3 * cols), jnp.bfloat16),
            pltpu.VMEM((depth, TILE, 3 * cols), jnp.bfloat16),
            pltpu.SemaphoreType.DMA((3,)),
            pltpu.SemaphoreType.DMA((depth, 2, 3)),
        ],
    )


def late_call(meta, near, low, chosen, sums, arrays, where, half, early, seq_len):
    cols, depth = near[0].shape[1], 3
    return matmul_call(
        lambda *refs: late_kernel(where, half, early, *refs),
        jax.ShapeDtypeStruct((seq_len, len(where) * TILE), jnp.bfloat16),
        (meta, *near, low, chosen, sums, *arrays),
        (1 + len(near), 4 + len(near)),
        [
            pltpu.VMEM((LIVE, 4 * cols), jnp.bfloat16),
            pltpu.VMEM((depth, TILE, 4 * cols), jnp.bfloat16),
            pltpu.SemaphoreType.DMA((4,)),
            pltpu.SemaphoreType.DMA((depth, 2, 4)),
        ],
    )


def gather_kernel(count, *refs):
    inputs, (out, buffer, come, go) = refs[:-4], refs[-4:]
    at, moves = 0, []
    for i, ref in enumerate(inputs):
        size = ref.shape[0]
        part = buffer.at[pl.ds(at, size)]
        arrive = pltpu.make_async_copy(ref, part, come.at[i])
        moves.append((arrive, pltpu.make_async_copy(part, out.at[pl.ds(at, size)], go.at[i])))
        arrive.start()
        at += size
    for arrive, leave in moves:
        arrive.wait()
        leave.start()
    for arrive, leave in moves:
        leave.wait()


def gather_pieces(arrays):
    spec = pl.BlockSpec(memory_space=pltpu.HBM)
    count = sum(array.shape[0] for array in arrays)
    shape = (count,) + arrays[0].shape[1:]
    return pl.pallas_call(
        lambda *refs: gather_kernel(count, *refs),
        out_shape=jax.ShapeDtypeStruct(shape, arrays[0].dtype),
        in_specs=[spec] * len(arrays),
        out_specs=spec,
        scratch_shapes=[
            pltpu.VMEM(shape, arrays[0].dtype),
            pltpu.SemaphoreType.DMA((len(arrays),)),
            pltpu.SemaphoreType.DMA((len(arrays),)),
        ],
        compiler_params=pltpu.CompilerParams(vmem_limit_bytes=32 * 2**20),
        cost_estimate=pl.CostEstimate(flops=0, transcendentals=0, bytes_accessed=0),
    )(*arrays)


def across(value):
    return lax.ppermute(value, "dp", [(i, i ^ 2) for i in range(4)])


def core(value):
    return lax.ppermute(value, "dp", [(i, i ^ 1) for i in range(4)])


def over(value):
    return lax.ppermute(value, "groups", [(0, 1), (1, 0)])


def line(value, step):
    def send(value, sign, far):
        pairs = [(i, i + 1) for i in range(far, 3)]
        return lax.ppermute(value, "fsdp", pairs if sign > 0 else [(3 - a, 3 - b) for a, b in pairs])

    return lambda sign: send(value, sign, step)


def turns(value):
    return [lax.ppermute(value, "fsdp", [(i, (i + k) % 4) for i in range(4)]) for k in (1, 2, 3)]


class Plan:
    def __init__(self, own, codes, scales, y):
        self.own, self.codes, self.scales = own, codes, scales.T
        self.pieces = codes.shape[0] // PIECE
        self.half = sum(SENT)
        self.group = y.astype(jnp.int32).reshape(1)
        self.up1, self.dn1 = line(own, 0)(1), line(own, 0)(-1)
        sent, direct = SENT[0], 2 * self.half
        (head,) = weight_pieces(
            self.group,
            codes,
            self.scales,
            lambda i: jnp.where(i < sent, i, direct),
            self.half,
            [(0, sent + 1)],
        )
        self.x0 = across(head)

    def sum_parts(self, parts):
        spans = [(0, self.pieces), (SENT[0], self.half), (2 * self.half + 1, self.pieces)]
        self.mine, first, self.direct = weight_pieces(
            after(self.group, parts), self.codes, self.scales, lambda i: i, self.half, spans
        )
        gathered = lax.all_gather(after(parts, self.mine), "fsdp", axis=0)
        ready = (gathered, self.x0, self.up1, self.dn1)
        self.x1 = across(after(first, *ready))
        self.y0 = over(after(self.x0[: SENT[0]], *ready))
        self.up2 = line(after(self.up1, *ready), 1)(1)
        self.dn2 = line(after(self.dn1, *ready), 1)(-1)
        self.sibling = core(after(self.mine, *ready))
        return [gathered]

    def gather_rows(self, row):
        rows = lax.all_gather(row, "dp", axis=0, tiled=True)
        done = (self.x1, self.y0, self.up2, self.dn2, rows, self.sibling)
        self.y1 = over(after(self.x1, *done))
        self.x2 = across(after(self.direct, *done))
        self.up3 = line(after(self.up2, *done), 2)(1)
        self.dn3 = line(after(self.dn2, *done), 2)(-1)
        self.far1 = gather_pieces(after((self.x0, self.x1, self.y0), *done))
        self.sib_far1 = core(self.far1)
        return after([rows], self.sib_far1)

    def finish(self, done, state_part, meta, low, chosen, seq_len):
        half, sent = self.half, SENT[0]
        near = [self.own, self.up1, self.dn1, self.up2, self.dn2]
        arrays = [self.mine, self.sibling, self.far1, self.sib_far1]

        far_at = {i: (2, i) for i in range(sent)}
        far_at[2 * half] = (2, sent)
        far_at.update({i: (2, 1 + i) for i in range(sent, half + sent)})
        far_at.update({half + sent + i: (4, i) for i in range(half - sent)})
        far_at.update({i: (6, i - 2 * half - 1) for i in range(2 * half + 1, self.pieces)})
        early_count = half + sent

        def entry(i):
            index, offset = far_at[i]
            return (i, ((0, i), (1, i), (index, offset), (index + 1, offset)))

        tiles = [(entry(i), entry(i + 1)) for i in range(0, self.pieces, 2)]
        early = early_count // 2
        sum1 = early_call(after(meta, done), low, chosen, near, arrays, tiles[:early], half)
        sib_y1 = core(after(self.y1, sum1))
        sib_x2 = core(after(self.x2, sib_y1, self.up3, self.dn3))
        others = turns(after(state_part, self.up3, self.dn3, sib_y1))
        arrays += [self.y1, sib_y1, self.x2, sib_x2]
        near += [self.up3, self.dn3]
        result = late_call(meta, near, low, chosen, sum1, arrays, tiles, half, early, seq_len)
        state_sum = state_part
        for other in others:
            state_sum = state_sum + after(other, result)
        return result, state_sum


def shards(
    hidden_in,
    cotangent,
    base_codes,
    base_scales,
    factor_a,
    factor_b,
    task_state,
    head_a,
    head_b,
    task_ids,
    valid_counts,
    owners,
):
    f32, bf16 = jnp.float32, jnp.bfloat16
    n_groups, n_fsdp, n_dp = (lax.axis_size(a) for a in ("groups", "fsdp", "dp"))
    z, p, y = (lax.axis_index(a) for a in ("fsdp", "dp", "groups"))
    seq_len, width_part = hidden_in.shape
    tasks_all, factor_cols = factor_a.shape
    rank_double = factor_cols // width_part
    rank_half = rank_double // 2
    joined_part = cotangent.shape[1]
    own = cotangent[:LIVE]
    lines = (n_groups, n_fsdp, n_dp) == (2, 4, 4) and width_part == 16 * PIECE
    plan = Plan(own, base_codes, base_scales, y) if lines else None

    task_rows = lax.broadcasted_iota(jnp.int32, (tasks_all, tasks_all), 0)
    task_other = lax.broadcasted_iota(jnp.int32, (tasks_all, tasks_all), 1)
    same_owner = owners[:, None] == owners[None, :]
    slot_index = jnp.sum((same_owner & (task_other < task_rows)).astype(jnp.int32), axis=1)
    target = owners * SLOTS + slot_index

    task = task_ids[0]
    chosen_a = lax.dynamic_slice_in_dim(factor_a, task, 1, 0).reshape(width_part, rank_double)
    chosen_b = lax.dynamic_slice_in_dim(factor_b, task, 1, 0).reshape(joined_part, rank_half)
    first_column = (z * joined_part).astype(jnp.int32).reshape(1)
    parts = whole_call(
        product_kernel,
        jax.ShapeDtypeStruct((LIVE, 2 * rank_double), bf16),
        hidden_in,
        cotangent,
        chosen_a,
        chosen_b,
        scalars=(first_column,),
    )
    if lines:
        parts = plan.sum_parts(parts)
    else:
        parts = [lax.all_gather(parts, "fsdp", axis=0)]
    scalars = jnp.stack([first_column[0], valid_counts[0]])
    down_gradient, up_gradient, low_grad = whole_call(
        factor_kernel,
        [
            jax.ShapeDtypeStruct((width_part, rank_double), f32),
            jax.ShapeDtypeStruct((joined_part, rank_half), f32),
            jax.ShapeDtypeStruct((LIVE, rank_double), bf16),
        ],
        hidden_in,
        cotangent,
        *parts,
        scalars=(scalars,),
    )
    down_cols = width_part * rank_double
    up_cols = joined_part * rank_half
    row = whole_call(
        row_kernel,
        jax.ShapeDtypeStruct((1, down_cols + up_cols + 128), bf16),
        down_gradient.astype(bf16).reshape(1, down_cols),
        up_gradient.astype(bf16).reshape(1, up_cols),
        jnp.full((1, 128), task, f32).astype(bf16),
    )
    rows = plan.gather_rows(row) if lines else [lax.all_gather(row, "dp", axis=0, tiled=True)]
    ids = jnp.concatenate([row[:, down_cols + up_cols] for row in rows]).astype(jnp.int32)
    one_hot = ids[:, None] == lax.broadcasted_iota(jnp.int32, (1, tasks_all), 1)
    states = jnp.dot(one_hot.astype(bf16), task_state, preferred_element_type=f32).astype(bf16)
    block = math.gcd(down_cols, up_cols)
    grad_head_b, part_b = head_grads(states, rows, head_b, down_cols, block)
    if lines:
        rows = after(rows, grad_head_b)
    grad_head_a, part_a = head_grads(states, rows, head_a, 0, block)
    state_part = part_a + part_b
    seq_target = jnp.sum(jnp.where(one_hot, target[None, :], 0), axis=1)
    own_rows = z * SLOTS + lax.broadcasted_iota(jnp.int32, (SLOTS, 1), 0)
    selector = (own_rows == seq_target[None, :]).astype(f32)
    if lines:
        done = (grad_head_a, grad_head_b, selector)
        meta = jnp.stack([z, p, y, valid_counts[0]]).astype(jnp.int32)
        input_gradient, state_sum = plan.finish(
            done, state_part, meta, low_grad, chosen_a, seq_len
        )
    else:
        state_sum = jnp.sum(lax.all_gather(state_part, "fsdp", axis=0), axis=0)
    grad_state = jnp.sum(selector[:, :, None] * state_sum[None, :, :], axis=1)

    if not lines:
        weight = dequantize(
            lax.all_gather(base_codes, "dp", axis=1, tiled=True),
            lax.all_gather(base_scales, "dp", axis=1, tiled=True),
        )
        merged = lax.dot_general(
            lax.all_gather(own, "fsdp", axis=1, tiled=True),
            weight,
            (((1,), (1,)), ((), ())),
            preferred_element_type=f32,
        )
        adapter = lax.dot_general(
            low_grad, chosen_a, (((1,), (1,)), ((), ())), preferred_element_type=f32
        )
        keep = lax.broadcasted_iota(jnp.int32, (LIVE, 1), 0) < valid_counts[0]
        live = (jnp.where(keep, merged, 0.0) + adapter_scale * adapter).astype(bf16)
        input_gradient = jnp.pad(live, ((0, seq_len - LIVE), (0, 0)))
    return (input_gradient, grad_head_a, grad_head_b, grad_state)


def solution(mesh):
    placed = (
        P(("groups", "dp"), "fsdp"),
        P(("groups", "dp"), "fsdp"),
        P("fsdp", "dp"),
        P("fsdp", "dp"),
        P("groups", "fsdp"),
        P("groups", "fsdp"),
        P("groups", "dp"),
        P("dp", "fsdp"),
        P("dp", "fsdp"),
        P(("groups", "dp")),
        P(("groups", "dp")),
        P("groups"),
    )
    return jax.shard_map(
        shards,
        mesh=mesh,
        in_specs=placed,
        out_specs=(
            P(("groups", "dp"), "fsdp"),
            P(("groups", "dp"), "fsdp"),
            P(("groups", "dp"), "fsdp"),
            P(("groups", "fsdp"), "dp"),
        ),
        check_vma=False,
    )
```

```python
import math

import jax
import jax.numpy as jnp
from jax import lax
from jax.experimental import pallas as pl
from jax.experimental.pallas import tpu as pltpu
from jax.sharding import PartitionSpec as P

HEADS = 64
KV_HEADS = 8
HEAD_DIM = 128
QBLOCK = 64
SLOTS = 4
LIVE = 384
TILE = 256
PIECE = 128
SENT = (3, 3)

adapter_scale = 2.0


def dequantize(codes, scales):
    rows, cols = codes.shape
    blocks = scales.shape[1]
    return (
        (
            codes.astype(jnp.float32).reshape(rows, blocks, QBLOCK)
            * scales.astype(jnp.float32)[:, :, None]
        )
        .reshape(rows, cols)
        .astype(jnp.bfloat16)
    )


def weight_kernel(spans, group, codes, scales, *outs):
    cols, blocks = codes.shape[1], scales.shape[0]
    spread = (
        lax.broadcasted_iota(jnp.int32, (blocks, cols), 1) // QBLOCK
        == lax.broadcasted_iota(jnp.int32, (blocks, cols), 0)
    ).astype(jnp.bfloat16)
    wide = lax.dot_general(
        scales[...], spread, (((0,), (0,)), ((), ())), preferred_element_type=jnp.float32
    )
    piece = (codes[...].astype(jnp.float32) * wide).astype(jnp.bfloat16)
    i = pl.program_id(0)
    for (low, high), out in zip(spans, outs):

        @pl.when((i >= low) & (i < high))
        def _(out=out):
            out[0] = piece


def placed_piece(at, group, half):
    moved = jnp.where(at < half, at + group * half, at - group * half)
    return jnp.where(at < 2 * half, moved, at)


def weight_pieces(group, codes, scales, half, spans):
    cols, blocks = codes.shape[1], scales.shape[0]
    count = spans[0][1]

    def span_spec(low, high):
        return pl.BlockSpec(
            (1, PIECE, cols), lambda i, group: (jnp.clip(i - low, 0, high - low - 1), 0, 0)
        )

    return pl.pallas_call(
        lambda *refs: weight_kernel(spans, *refs),
        out_shape=[
            jax.ShapeDtypeStruct((high - low, PIECE, cols), jnp.bfloat16) for low, high in spans
        ],
        grid_spec=pltpu.PrefetchScalarGridSpec(
            num_scalar_prefetch=1,
            grid=(count,),
            in_specs=[
                pl.BlockSpec(
                    (PIECE, cols), lambda i, group: (placed_piece(i, group[0], half), 0)
                ),
                pl.BlockSpec(
                    (blocks, PIECE), lambda i, group: (0, placed_piece(i, group[0], half))
                ),
            ],
            out_specs=[span_spec(low, high) for low, high in spans],
        ),
        compiler_params=pltpu.CompilerParams(vmem_limit_bytes=32 * 2**20),
        cost_estimate=pl.CostEstimate(flops=0, transcendentals=0, bytes_accessed=0),
    )(group, codes, scales)


def value_columns(first, count):
    group_cols = (HEADS // KV_HEADS + 1) * HEAD_DIM
    column = first + lax.broadcasted_iota(jnp.int32, (count, 1), 0)
    return lax.rem(column, group_cols) >= HEADS // KV_HEADS * HEAD_DIM


def product_kernel(first, hidden, cotangent, chosen_a, chosen_b, out):
    value = value_columns(first[0], cotangent.shape[1])
    plain = chosen_b[...]
    empty = jnp.zeros_like(plain)
    joined = jnp.concatenate(
        [jnp.where(value, empty, plain), jnp.where(value, plain, empty)], axis=1
    )
    inner = jnp.dot(hidden[:LIVE, :], chosen_a[...], preferred_element_type=jnp.float32)
    outer = jnp.dot(cotangent[:LIVE, :], joined, preferred_element_type=jnp.float32)
    out[...] = jnp.concatenate([inner, outer], axis=1).astype(out.dtype)


def factor_kernel(scalars, hidden, cotangent, parts, down, up, low_grad):
    rank = low_grad.shape[1]
    total = parts[0].astype(jnp.float32)
    for i in range(1, parts.shape[0]):
        total = total + parts[i].astype(jnp.float32)
    keep = lax.broadcasted_iota(jnp.int32, (LIVE, 1), 0) < scalars[1]
    sums = jnp.where(keep, total, 0.0).astype(jnp.bfloat16)
    low, grad = sums[:, :rank], sums[:, rank:]
    low_grad[...] = grad
    contract = (((0,), (0,)), ((), ()))
    down[...] = adapter_scale * lax.dot_general(
        hidden[:LIVE, :], grad, contract, preferred_element_type=jnp.float32
    )
    mixed = lax.dot_general(
        cotangent[:LIVE, :], low, contract, preferred_element_type=jnp.float32
    )
    half = rank // 2
    value = value_columns(scalars[0], cotangent.shape[1])
    up[...] = adapter_scale * jnp.where(value, mixed[:, half:], mixed[:, :half])


def row_kernel(down, up, task, out):
    down_cols, up_cols = down.shape[1], up.shape[1]
    out[:, :down_cols] = down[...]
    out[:, down_cols : down_cols + up_cols] = up[...]
    out[:, down_cols + up_cols :] = task[...]


def head_kernel(states, *refs):
    head, grad, part = refs[-3:]
    rows = jnp.concatenate([ref[...] for ref in refs[:-3]], axis=0)
    grad[...] = lax.dot_general(
        states[...], rows, (((0,), (0,)), ((), ())), preferred_element_type=jnp.float32
    )

    @pl.when(pl.program_id(0) == 0)
    def _():
        part[...] = jnp.zeros_like(part)

    part[...] += lax.dot_general(
        rows, head[...], (((1,), (1,)), ((), ())), preferred_element_type=jnp.float32
    )


def head_grads(states, rows, head, first, block):
    hidden_units, cols = head.shape
    sequences = sum(row.shape[0] for row in rows)
    return pl.pallas_call(
        head_kernel,
        out_shape=[
            jax.ShapeDtypeStruct((hidden_units, cols), jnp.float32),
            jax.ShapeDtypeStruct((sequences, hidden_units), jnp.float32),
        ],
        grid=(cols // block,),
        in_specs=[
            pl.BlockSpec((sequences, hidden_units), lambda i: (0, 0)),
        ]
        + [pl.BlockSpec((row.shape[0], block), lambda i: (0, first // block + i)) for row in rows]
        + [pl.BlockSpec((hidden_units, block), lambda i: (0, i))],
        out_specs=[
            pl.BlockSpec((hidden_units, block), lambda i: (0, i)),
            pl.BlockSpec((sequences, hidden_units), lambda i: (0, 0)),
        ],
        compiler_params=pltpu.CompilerParams(vmem_limit_bytes=32 * 2**20),
        cost_estimate=pl.CostEstimate(flops=0, transcendentals=0, bytes_accessed=0),
    )(states, *rows, head)


def whole_call(kernel, out_shape, *operands, scalars=()):
    spec = pl.BlockSpec(memory_space=pltpu.VMEM)
    return pl.pallas_call(
        kernel,
        out_shape=out_shape,
        in_specs=[pl.BlockSpec(memory_space=pltpu.SMEM)] * len(scalars) + [spec] * len(operands),
        out_specs=jax.tree.map(lambda _: spec, out_shape),
        compiler_params=pltpu.CompilerParams(vmem_limit_bytes=32 * 2**20),
        cost_estimate=pl.CostEstimate(flops=0, transcendentals=0, bytes_accessed=0),
    )(*scalars, *operands)


def after(value, *done):
    return lax.optimization_barrier((value, done))[0]


def last_slot(z):
    return jnp.where(z == 0, 1, jnp.where(z == 3, 3, 2))


def order_of(slot, last):
    return jnp.where(slot == last, 3, jnp.where(slot < last, slot, slot - 1))


def start_copy(condition, source, target, sem):
    pl.when(condition)(lambda: pltpu.make_async_copy(source, target, sem).start())


def early_kernel(where, half, *refs):
    meta, low, chosen, own, up1, dn1, up2, dn2 = refs[:8]
    arrays, (out, cot, wbuf, csem, wsem) = refs[8:-5], refs[-5:]
    z, p, y, valid = meta[0], meta[1], meta[2], meta[3]
    depth, cols, tiles = wbuf.shape[0], own.shape[1], len(where)
    last = last_slot(z)

    def send(tile, slot):
        for side in range(2):
            for j in range(4):
                index, offset = where[tile][side][1][j]
                back = jnp.bitwise_and(z - jnp.bitwise_xor(p, j), 3)
                place = order_of(back, last)
                at = pl.multiple_of(jnp.minimum(place, 2) * cols, 128)
                start_copy(
                    back != last,
                    arrays[index].at[offset],
                    wbuf.at[slot, pl.ds(side * PIECE, PIECE), pl.ds(at, cols)],
                    wsem.at[slot, side, jnp.minimum(place, 2)],
                )

    for slot in range(min(depth - 1, tiles)):
        send(slot, slot)
    part = lambda place: cot.at[:, pl.ds(place * cols, cols)]
    start_copy(z >= 0, own, part(0), csem.at[0])
    start_copy(z == 0, dn2, part(1), csem.at[1])
    start_copy(z >= 1, up1, part(1), csem.at[1])
    start_copy(z <= 2, dn1, part(2), csem.at[2])
    start_copy(z == 3, up2, part(2), csem.at[2])
    keep = lax.broadcasted_iota(jnp.int32, (LIVE, 1), 0) < valid
    rows = (((1,), (1,)), ((), ()))
    for place in range(3):
        pltpu.make_async_copy(own, part(place), csem.at[place]).wait()

    @pl.loop(0, tiles)
    def _(tile):
        slot = lax.rem(tile, depth)
        for index in range(depth - 1, tiles):
            pl.when(tile + depth - 1 == index)(lambda index=index: send(index, index % depth))
        for side in range(2):
            for place in range(3):
                target = wbuf.at[slot, pl.ds(side * PIECE, PIECE), pl.ds(place * cols, cols)]
                pltpu.make_async_copy(target, target, wsem.at[slot, side, place]).wait()
        total = lax.dot_general(cot[...], wbuf[slot], rows, preferred_element_type=jnp.float32)
        for side in range(2):
            start = pl.multiple_of(placed_piece(2 * tile + side, y, half) * PIECE, PIECE)
            adapter = adapter_scale * lax.dot_general(
                low[...], chosen[pl.ds(start, PIECE), :], rows, preferred_element_type=jnp.float32
            )
            piece = total[:, side * PIECE : (side + 1) * PIECE]
            at = pl.multiple_of(tile * TILE + side * PIECE, PIECE)
            out[:, pl.ds(at, PIECE)] = jnp.where(keep, piece, 0.0) + adapter


def late_kernel(where, half, early, *refs):
    meta, own, up1, dn1, up2, dn2, up3, dn3, low, chosen, sums = refs[:11]
    arrays, (out, cot, wbuf, csem, wsem) = refs[11:-5], refs[-5:]
    z, p, y, valid = meta[0], meta[1], meta[2], meta[3]
    depth, cols, tiles = wbuf.shape[0], own.shape[1], len(where)
    last = last_slot(z)

    def send(tile, slot):
        for side in range(2):
            for j in range(4):
                index, offset = where[tile][side][1][j]
                back = jnp.bitwise_and(z - jnp.bitwise_xor(p, j), 3)
                place = order_of(back, last)
                start_copy(
                    (back == last) if tile < early else (back >= 0),
                    arrays[index].at[offset],
                    wbuf.at[
                        slot,
                        pl.ds(side * PIECE, PIECE),
                        pl.ds(pl.multiple_of(place * cols, 128), cols),
                    ],
                    wsem.at[slot, side, place],
                )

    part = lambda place: cot.at[:, pl.ds(place * cols, cols)]
    start_copy(z == 0, dn3, part(3), csem.at[3])
    start_copy(z == 1, dn2, part(3), csem.at[3])
    start_copy(z == 2, up2, part(3), csem.at[3])
    start_copy(z == 3, up3, part(3), csem.at[3])
    for slot in range(depth - 1):
        send(slot, slot)
    start_copy(z >= 0, own, part(0), csem.at[0])
    start_copy(z == 0, dn2, part(1), csem.at[1])
    start_copy(z >= 1, up1, part(1), csem.at[1])
    start_copy(z <= 2, dn1, part(2), csem.at[2])
    start_copy(z == 3, up2, part(2), csem.at[2])
    keep = lax.broadcasted_iota(jnp.int32, (LIVE, 1), 0) < valid
    rows = (((1,), (1,)), ((), ()))
    out[LIVE:, :] = jnp.zeros((out.shape[0] - LIVE, out.shape[1]), out.dtype)
    pltpu.make_async_copy(part(3), part(3), csem.at[3]).wait()

    def product(tile, first):
        slot = lax.rem(tile, depth)
        for index in range(depth - 1, tiles):
            pl.when(tile + depth - 1 == index)(lambda index=index: send(index, index % depth))
        for side in range(2):
            for place in range(first, 4):
                target = wbuf.at[slot, pl.ds(side * PIECE, PIECE), pl.ds(place * cols, cols)]
                pltpu.make_async_copy(target, target, wsem.at[slot, side, place]).wait()
        return lax.dot_general(
            cot[:, first * cols :],
            wbuf[slot, :, first * cols :],
            rows,
            preferred_element_type=jnp.float32,
        )

    def store(tile, side, total, before):
        start = pl.multiple_of(placed_piece(2 * tile + side, y, half) * PIECE, PIECE)
        piece = jnp.where(keep, total[:, side * PIECE : (side + 1) * PIECE], 0.0)
        out[:LIVE, pl.ds(start, PIECE)] = (before(start) + piece).astype(out.dtype)

    @pl.loop(0, early)
    def _(tile):
        total = product(tile, 3)
        for side in range(2):
            at = pl.multiple_of(tile * TILE + side * PIECE, PIECE)
            store(tile, side, total, lambda start: sums[:, pl.ds(at, PIECE)])

    for place in range(3):
        pltpu.make_async_copy(part(place), part(place), csem.at[place]).wait()

    def adapter(start):
        return adapter_scale * lax.dot_general(
            low[...], chosen[pl.ds(start, PIECE), :], rows, preferred_element_type=jnp.float32
        )

    @pl.loop(early, tiles)
    def _(tile):
        total = product(tile, 0)
        for side in range(2):
            store(tile, side, total, adapter)


def matmul_call(kernel, out_shape, operands, vmem_count, scratch):
    smem = pl.BlockSpec(memory_space=pltpu.SMEM)
    vmem = pl.BlockSpec(memory_space=pltpu.VMEM)
    hbm = pl.BlockSpec(memory_space=pltpu.HBM)
    first, last = vmem_count
    specs = [smem] + [
        vmem if first <= i < last else hbm for i in range(1, len(operands))
    ]
    return pl.pallas_call(
        kernel,
        out_shape=out_shape,
        in_specs=specs,
        out_specs=vmem,
        scratch_shapes=scratch,
        compiler_params=pltpu.CompilerParams(vmem_limit_bytes=44 * 2**20),
        cost_estimate=pl.CostEstimate(flops=0, transcendentals=0, bytes_accessed=0),
    )(*operands)


def early_call(meta, low, chosen, near, arrays, where, half):
    cols, depth = near[0].shape[1], 3
    return matmul_call(
        lambda *refs: early_kernel(where, half, *refs),
        jax.ShapeDtypeStruct((LIVE, len(where) * TILE), jnp.float32),
        (meta, low, chosen, *near, *arrays),
        (1, 3),
        [
            pltpu.VMEM((LIVE, 3 * cols), jnp.bfloat16),
            pltpu.VMEM((depth, TILE, 3 * cols), jnp.bfloat16),
            pltpu.SemaphoreType.DMA((3,)),
            pltpu.SemaphoreType.DMA((depth, 2, 3)),
        ],
    )


def late_call(meta, near, low, chosen, sums, arrays, where, half, early, seq_len):
    cols, depth = near[0].shape[1], 3
    return matmul_call(
        lambda *refs: late_kernel(where, half, early, *refs),
        jax.ShapeDtypeStruct((seq_len, len(where) * TILE), jnp.bfloat16),
        (meta, *near, low, chosen, sums, *arrays),
        (1 + len(near), 4 + len(near)),
        [
            pltpu.VMEM((LIVE, 4 * cols), jnp.bfloat16),
            pltpu.VMEM((depth, TILE, 4 * cols), jnp.bfloat16),
            pltpu.SemaphoreType.DMA((4,)),
            pltpu.SemaphoreType.DMA((depth, 2, 4)),
        ],
    )


def gather_kernel(count, *refs):
    inputs, (out, buffer, come, go) = refs[:-4], refs[-4:]
    at, moves = 0, []
    for i, ref in enumerate(inputs):
        size = ref.shape[0]
        part = buffer.at[pl.ds(at, size)]
        arrive = pltpu.make_async_copy(ref, part, come.at[i])
        moves.append((arrive, pltpu.make_async_copy(part, out.at[pl.ds(at, size)], go.at[i])))
        arrive.start()
        at += size
    for arrive, leave in moves:
        arrive.wait()
        leave.start()
    for arrive, leave in moves:
        leave.wait()


def gather_pieces(arrays):
    spec = pl.BlockSpec(memory_space=pltpu.HBM)
    count = sum(array.shape[0] for array in arrays)
    shape = (count,) + arrays[0].shape[1:]
    return pl.pallas_call(
        lambda *refs: gather_kernel(count, *refs),
        out_shape=jax.ShapeDtypeStruct(shape, arrays[0].dtype),
        in_specs=[spec] * len(arrays),
        out_specs=spec,
        scratch_shapes=[
            pltpu.VMEM(shape, arrays[0].dtype),
            pltpu.SemaphoreType.DMA((len(arrays),)),
            pltpu.SemaphoreType.DMA((len(arrays),)),
        ],
        compiler_params=pltpu.CompilerParams(vmem_limit_bytes=32 * 2**20),
        cost_estimate=pl.CostEstimate(flops=0, transcendentals=0, bytes_accessed=0),
    )(*arrays)


def across(value):
    return lax.ppermute(value, "dp", [(i, i ^ 2) for i in range(4)])


def core(value):
    return lax.ppermute(value, "dp", [(i, i ^ 1) for i in range(4)])


def over(value):
    return lax.ppermute(value, "groups", [(0, 1), (1, 0)])


def line(value, step):
    def send(value, sign, far):
        pairs = [(i, i + 1) for i in range(far, 3)]
        return lax.ppermute(value, "fsdp", pairs if sign > 0 else [(3 - a, 3 - b) for a, b in pairs])

    return lambda sign: send(value, sign, step)


def turns(value):
    return [lax.ppermute(value, "fsdp", [(i, (i + k) % 4) for i in range(4)]) for k in (1, 2, 3)]


class Plan:
    def __init__(self, own, codes, scales, y):
        self.own, self.codes, self.scales = own, codes, scales.T
        self.pieces = codes.shape[0] // PIECE
        self.half = sum(SENT)
        self.group = y.astype(jnp.int32).reshape(1)
        self.up1, self.dn1 = line(own, 0)(1), line(own, 0)(-1)
        (head,) = weight_pieces(self.group, codes, self.scales, self.half, [(0, SENT[0])])
        self.x0 = across(head)

    def sum_parts(self, parts):
        spans = [(0, self.pieces), (SENT[0], self.half), (2 * self.half, self.pieces)]
        self.mine, first, self.direct = weight_pieces(
            after(self.group, parts), self.codes, self.scales, self.half, spans
        )
        gathered = lax.all_gather(after(parts, self.mine), "fsdp", axis=0)
        ready = (gathered, self.up1, self.dn1)
        self.x1 = across(after(first, *ready))
        self.y0 = over(after(self.x0, *ready))
        self.up2 = line(after(self.up1, *ready), 1)(1)
        self.dn2 = line(after(self.dn1, *ready), 1)(-1)
        self.sibling = core(after(self.mine, *ready, self.x0))
        return [gathered]

    def gather_rows(self, row):
        rows = lax.all_gather(row, "dp", axis=0, tiled=True)
        done = (self.x1, self.y0, self.up2, self.dn2, rows, self.sibling)
        self.y1 = over(after(self.x1, *done))
        self.x2 = across(after(self.direct, *done))
        self.up3 = line(after(self.up2, *done), 2)(1)
        self.dn3 = line(after(self.dn2, *done), 2)(-1)
        self.far1 = gather_pieces(after((self.x0, self.x1, self.y0), *done))
        self.sib_far1 = core(self.far1)
        return after([rows], self.sib_far1)

    def finish(self, done, state_part, meta, low, chosen, seq_len):
        half, sent = self.half, SENT[0]
        near = [self.own, self.up1, self.dn1, self.up2, self.dn2]
        arrays = [self.mine, self.sibling, self.far1, self.sib_far1]

        far_at = {i: (2, i) for i in range(half + sent)}
        far_at.update({half + sent + i: (4, i) for i in range(half - sent)})
        far_at.update({i: (6, i - 2 * half) for i in range(2 * half, self.pieces)})
        early_count = half + sent

        def entry(i):
            index, offset = far_at[i]
            return (i, ((0, i), (1, i), (index, offset), (index + 1, offset)))

        tiles = [(entry(i), entry(i + 1)) for i in range(0, self.pieces, 2)]
        early = early_count // 2
        sum1 = early_call(after(meta, done), low, chosen, near, arrays, tiles[:early], half)
        sib_y1 = core(after(self.y1, sum1))
        sib_x2 = core(after(self.x2, sib_y1, self.up3, self.dn3))
        others = turns(after(state_part, self.up3, self.dn3, sib_y1))
        arrays += [self.y1, sib_y1, self.x2, sib_x2]
        near += [self.up3, self.dn3]
        result = late_call(meta, near, low, chosen, sum1, arrays, tiles, half, early, seq_len)
        state_sum = state_part
        for other in others:
            state_sum = state_sum + after(other, result)
        return result, state_sum


def shards(
    hidden_in,
    cotangent,
    base_codes,
    base_scales,
    factor_a,
    factor_b,
    task_state,
    head_a,
    head_b,
    task_ids,
    valid_counts,
    owners,
):
    f32, bf16 = jnp.float32, jnp.bfloat16
    n_groups, n_fsdp, n_dp = (lax.axis_size(a) for a in ("groups", "fsdp", "dp"))
    z, p, y = (lax.axis_index(a) for a in ("fsdp", "dp", "groups"))
    seq_len, width_part = hidden_in.shape
    tasks_all, factor_cols = factor_a.shape
    rank_double = factor_cols // width_part
    rank_half = rank_double // 2
    joined_part = cotangent.shape[1]
    own = cotangent[:LIVE]
    lines = (n_groups, n_fsdp, n_dp) == (2, 4, 4) and width_part == 16 * PIECE
    plan = Plan(own, base_codes, base_scales, y) if lines else None

    task_rows = lax.broadcasted_iota(jnp.int32, (tasks_all, tasks_all), 0)
    task_other = lax.broadcasted_iota(jnp.int32, (tasks_all, tasks_all), 1)
    same_owner = owners[:, None] == owners[None, :]
    slot_index = jnp.sum((same_owner & (task_other < task_rows)).astype(jnp.int32), axis=1)
    target = owners * SLOTS + slot_index

    task = task_ids[0]
    chosen_a = lax.dynamic_slice_in_dim(factor_a, task, 1, 0).reshape(width_part, rank_double)
    chosen_b = lax.dynamic_slice_in_dim(factor_b, task, 1, 0).reshape(joined_part, rank_half)
    first_column = (z * joined_part).astype(jnp.int32).reshape(1)
    parts = whole_call(
        product_kernel,
        jax.ShapeDtypeStruct((LIVE, 2 * rank_double), bf16),
        hidden_in,
        cotangent,
        chosen_a,
        chosen_b,
        scalars=(first_column,),
    )
    if lines:
        parts = plan.sum_parts(parts)
    else:
        parts = [lax.all_gather(parts, "fsdp", axis=0)]
    scalars = jnp.stack([first_column[0], valid_counts[0]])
    down_gradient, up_gradient, low_grad = whole_call(
        factor_kernel,
        [
            jax.ShapeDtypeStruct((width_part, rank_double), f32),
            jax.ShapeDtypeStruct((joined_part, rank_half), f32),
            jax.ShapeDtypeStruct((LIVE, rank_double), bf16),
        ],
        hidden_in,
        cotangent,
        *parts,
        scalars=(scalars,),
    )
    down_cols = width_part * rank_double
    up_cols = joined_part * rank_half
    row = whole_call(
        row_kernel,
        jax.ShapeDtypeStruct((1, down_cols + up_cols + 128), bf16),
        down_gradient.astype(bf16).reshape(1, down_cols),
        up_gradient.astype(bf16).reshape(1, up_cols),
        jnp.full((1, 128), task, f32).astype(bf16),
    )
    rows = plan.gather_rows(row) if lines else [lax.all_gather(row, "dp", axis=0, tiled=True)]
    ids = jnp.concatenate([row[:, down_cols + up_cols] for row in rows]).astype(jnp.int32)
    one_hot = ids[:, None] == lax.broadcasted_iota(jnp.int32, (1, tasks_all), 1)
    states = jnp.dot(one_hot.astype(bf16), task_state, preferred_element_type=f32).astype(bf16)
    block = math.gcd(down_cols, up_cols)
    grad_head_b, part_b = head_grads(states, rows, head_b, down_cols, block)
    if lines:
        rows = after(rows, grad_head_b)
    grad_head_a, part_a = head_grads(states, rows, head_a, 0, block)
    state_part = part_a + part_b
    seq_target = jnp.sum(jnp.where(one_hot, target[None, :], 0), axis=1)
    own_rows = z * SLOTS + lax.broadcasted_iota(jnp.int32, (SLOTS, 1), 0)
    selector = (own_rows == seq_target[None, :]).astype(f32)
    if lines:
        done = (grad_head_a, grad_head_b, selector)
        meta = jnp.stack([z, p, y, valid_counts[0]]).astype(jnp.int32)
        input_gradient, state_sum = plan.finish(
            done, state_part, meta, low_grad, chosen_a, seq_len
        )
    else:
        state_sum = jnp.sum(lax.all_gather(state_part, "fsdp", axis=0), axis=0)
    grad_state = jnp.sum(selector[:, :, None] * state_sum[None, :, :], axis=1)

    if not lines:
        weight = dequantize(
            lax.all_gather(base_codes, "dp", axis=1, tiled=True),
            lax.all_gather(base_scales, "dp", axis=1, tiled=True),
        )
        merged = lax.dot_general(
            lax.all_gather(own, "fsdp", axis=1, tiled=True),
            weight,
            (((1,), (1,)), ((), ())),
            preferred_element_type=f32,
        )
        adapter = lax.dot_general(
            low_grad, chosen_a, (((1,), (1,)), ((), ())), preferred_element_type=f32
        )
        keep = lax.broadcasted_iota(jnp.int32, (LIVE, 1), 0) < valid_counts[0]
        live = (jnp.where(keep, merged, 0.0) + adapter_scale * adapter).astype(bf16)
        input_gradient = jnp.pad(live, ((0, seq_len - LIVE), (0, 0)))
    return (input_gradient, grad_head_a, grad_head_b, grad_state)


def solution(mesh):
    placed = (
        P(("groups", "dp"), "fsdp"),
        P(("groups", "dp"), "fsdp"),
        P("fsdp", "dp"),
        P("fsdp", "dp"),
        P("groups", "fsdp"),
        P("groups", "fsdp"),
        P("groups", "dp"),
        P("dp", "fsdp"),
        P("dp", "fsdp"),
        P(("groups", "dp")),
        P(("groups", "dp")),
        P("groups"),
    )
    return jax.shard_map(
        shards,
        mesh=mesh,
        in_specs=placed,
        out_specs=(
            P(("groups", "dp"), "fsdp"),
            P(("groups", "dp"), "fsdp"),
            P(("groups", "dp"), "fsdp"),
            P(("groups", "fsdp"), "dp"),
        ),
        check_vma=False,
    )
```

```python
import math

import jax
import jax.numpy as jnp
from jax import lax
from jax.experimental import pallas as pl
from jax.experimental.pallas import tpu as pltpu
from jax.sharding import PartitionSpec as P

HEADS = 64
KV_HEADS = 8
HEAD_DIM = 128
QBLOCK = 64
SLOTS = 4
LIVE = 384
TILE = 256
PIECE = 128
SENT = (3, 3)

adapter_scale = 2.0


def dequantize(codes, scales):
    rows, cols = codes.shape
    blocks = scales.shape[1]
    return (
        (
            codes.astype(jnp.float32).reshape(rows, blocks, QBLOCK)
            * scales.astype(jnp.float32)[:, :, None]
        )
        .reshape(rows, cols)
        .astype(jnp.bfloat16)
    )


def weight_kernel(spans, group, codes, scales, *outs):
    cols, blocks = codes.shape[1], scales.shape[0]
    spread = (
        lax.broadcasted_iota(jnp.int32, (blocks, cols), 1) // QBLOCK
        == lax.broadcasted_iota(jnp.int32, (blocks, cols), 0)
    ).astype(jnp.bfloat16)
    wide = lax.dot_general(
        scales[...], spread, (((0,), (0,)), ((), ())), preferred_element_type=jnp.float32
    )
    piece = (codes[...].astype(jnp.float32) * wide).astype(jnp.bfloat16)
    i = pl.program_id(0)
    for (low, high), out in zip(spans, outs):

        @pl.when((i >= low) & (i < high))
        def _(out=out):
            out[0] = piece


def placed_piece(at, group, half):
    moved = jnp.where(at < half, at + group * half, at - group * half)
    return jnp.where(at < 2 * half, moved, at)


def weight_pieces(group, codes, scales, half, spans):
    cols, blocks = codes.shape[1], scales.shape[0]
    count = spans[0][1]

    def span_spec(low, high):
        return pl.BlockSpec(
            (1, PIECE, cols), lambda i, group: (jnp.clip(i - low, 0, high - low - 1), 0, 0)
        )

    return pl.pallas_call(
        lambda *refs: weight_kernel(spans, *refs),
        out_shape=[
            jax.ShapeDtypeStruct((high - low, PIECE, cols), jnp.bfloat16) for low, high in spans
        ],
        grid_spec=pltpu.PrefetchScalarGridSpec(
            num_scalar_prefetch=1,
            grid=(count,),
            in_specs=[
                pl.BlockSpec(
                    (PIECE, cols), lambda i, group: (placed_piece(i, group[0], half), 0)
                ),
                pl.BlockSpec(
                    (blocks, PIECE), lambda i, group: (0, placed_piece(i, group[0], half))
                ),
            ],
            out_specs=[span_spec(low, high) for low, high in spans],
        ),
        compiler_params=pltpu.CompilerParams(vmem_limit_bytes=32 * 2**20),
        cost_estimate=pl.CostEstimate(flops=0, transcendentals=0, bytes_accessed=0),
    )(group, codes, scales)


def value_columns(first, count):
    group_cols = (HEADS // KV_HEADS + 1) * HEAD_DIM
    column = first + lax.broadcasted_iota(jnp.int32, (count, 1), 0)
    return lax.rem(column, group_cols) >= HEADS // KV_HEADS * HEAD_DIM


def product_kernel(first, hidden, cotangent, chosen_a, chosen_b, out):
    value = value_columns(first[0], cotangent.shape[1])
    plain = chosen_b[...]
    empty = jnp.zeros_like(plain)
    joined = jnp.concatenate(
        [jnp.where(value, empty, plain), jnp.where(value, plain, empty)], axis=1
    )
    inner = jnp.dot(hidden[:LIVE, :], chosen_a[...], preferred_element_type=jnp.float32)
    outer = jnp.dot(cotangent[:LIVE, :], joined, preferred_element_type=jnp.float32)
    out[...] = jnp.concatenate([inner, outer], axis=1).astype(out.dtype)


def factor_kernel(scalars, hidden, cotangent, parts, down, up, low_grad):
    rank = low_grad.shape[1]
    total = parts[0].astype(jnp.float32)
    for i in range(1, parts.shape[0]):
        total = total + parts[i].astype(jnp.float32)
    keep = lax.broadcasted_iota(jnp.int32, (LIVE, 1), 0) < scalars[1]
    sums = jnp.where(keep, total, 0.0).astype(jnp.bfloat16)
    low, grad = sums[:, :rank], sums[:, rank:]
    low_grad[...] = grad
    contract = (((0,), (0,)), ((), ()))
    down[...] = adapter_scale * lax.dot_general(
        hidden[:LIVE, :], grad, contract, preferred_element_type=jnp.float32
    )
    mixed = lax.dot_general(
        cotangent[:LIVE, :], low, contract, preferred_element_type=jnp.float32
    )
    half = rank // 2
    value = value_columns(scalars[0], cotangent.shape[1])
    up[...] = adapter_scale * jnp.where(value, mixed[:, half:], mixed[:, :half])


def row_kernel(down, up, task, out):
    down_cols, up_cols = down.shape[1], up.shape[1]
    out[:, :down_cols] = down[...]
    out[:, down_cols : down_cols + up_cols] = up[...]
    out[:, down_cols + up_cols :] = task[...]


def head_kernel(states, *refs):
    head, grad, part = refs[-3:]
    rows = jnp.concatenate([ref[...] for ref in refs[:-3]], axis=0)
    grad[...] = lax.dot_general(
        states[...], rows, (((0,), (0,)), ((), ())), preferred_element_type=jnp.float32
    )

    @pl.when(pl.program_id(0) == 0)
    def _():
        part[...] = jnp.zeros_like(part)

    part[...] += lax.dot_general(
        rows, head[...], (((1,), (1,)), ((), ())), preferred_element_type=jnp.float32
    )


def head_grads(states, rows, head, first, block):
    hidden_units, cols = head.shape
    sequences = sum(row.shape[0] for row in rows)
    return pl.pallas_call(
        head_kernel,
        out_shape=[
            jax.ShapeDtypeStruct((hidden_units, cols), jnp.float32),
            jax.ShapeDtypeStruct((sequences, hidden_units), jnp.float32),
        ],
        grid=(cols // block,),
        in_specs=[
            pl.BlockSpec((sequences, hidden_units), lambda i: (0, 0)),
        ]
        + [pl.BlockSpec((row.shape[0], block), lambda i: (0, first // block + i)) for row in rows]
        + [pl.BlockSpec((hidden_units, block), lambda i: (0, i))],
        out_specs=[
            pl.BlockSpec((hidden_units, block), lambda i: (0, i)),
            pl.BlockSpec((sequences, hidden_units), lambda i: (0, 0)),
        ],
        compiler_params=pltpu.CompilerParams(vmem_limit_bytes=32 * 2**20),
        cost_estimate=pl.CostEstimate(flops=0, transcendentals=0, bytes_accessed=0),
    )(states, *rows, head)


def whole_call(kernel, out_shape, *operands, scalars=()):
    spec = pl.BlockSpec(memory_space=pltpu.VMEM)
    return pl.pallas_call(
        kernel,
        out_shape=out_shape,
        in_specs=[pl.BlockSpec(memory_space=pltpu.SMEM)] * len(scalars) + [spec] * len(operands),
        out_specs=jax.tree.map(lambda _: spec, out_shape),
        compiler_params=pltpu.CompilerParams(vmem_limit_bytes=32 * 2**20),
        cost_estimate=pl.CostEstimate(flops=0, transcendentals=0, bytes_accessed=0),
    )(*scalars, *operands)


def after(value, *done):
    return lax.optimization_barrier((value, done))[0]


def last_slot(z):
    return jnp.where(z == 0, 1, jnp.where(z == 3, 3, 2))


def order_of(slot, last):
    return jnp.where(slot == last, 3, jnp.where(slot < last, slot, slot - 1))


def start_copy(condition, source, target, sem):
    pl.when(condition)(lambda: pltpu.make_async_copy(source, target, sem).start())


def early_kernel(where, half, *refs):
    meta, low, chosen, own, up1, dn1, up2, dn2 = refs[:8]
    arrays, (out, cot, wbuf, csem, wsem) = refs[8:-5], refs[-5:]
    z, p, y, valid = meta[0], meta[1], meta[2], meta[3]
    depth, cols, tiles = wbuf.shape[0], own.shape[1], len(where)
    last = last_slot(z)

    def send(tile, slot):
        for side in range(2):
            for j in range(4):
                index, offset = where[tile][side][1][j]
                back = jnp.bitwise_and(z - jnp.bitwise_xor(p, j), 3)
                place = order_of(back, last)
                at = pl.multiple_of(jnp.minimum(place, 2) * cols, 128)
                start_copy(
                    back != last,
                    arrays[index].at[offset],
                    wbuf.at[slot, pl.ds(side * PIECE, PIECE), pl.ds(at, cols)],
                    wsem.at[slot, side, jnp.minimum(place, 2)],
                )

    for slot in range(min(depth - 1, tiles)):
        send(slot, slot)
    part = lambda place: cot.at[:, pl.ds(place * cols, cols)]
    start_copy(z >= 0, own, part(0), csem.at[0])
    start_copy(z == 0, dn2, part(1), csem.at[1])
    start_copy(z >= 1, up1, part(1), csem.at[1])
    start_copy(z <= 2, dn1, part(2), csem.at[2])
    start_copy(z == 3, up2, part(2), csem.at[2])
    keep = lax.broadcasted_iota(jnp.int32, (LIVE, 1), 0) < valid
    rows = (((1,), (1,)), ((), ()))
    for place in range(3):
        pltpu.make_async_copy(own, part(place), csem.at[place]).wait()

    @pl.loop(0, tiles)
    def _(tile):
        slot = lax.rem(tile, depth)
        for index in range(depth - 1, tiles):
            pl.when(tile + depth - 1 == index)(lambda index=index: send(index, index % depth))
        for side in range(2):
            for place in range(3):
                target = wbuf.at[slot, pl.ds(side * PIECE, PIECE), pl.ds(place * cols, cols)]
                pltpu.make_async_copy(target, target, wsem.at[slot, side, place]).wait()
        total = lax.dot_general(cot[...], wbuf[slot], rows, preferred_element_type=jnp.float32)
        for side in range(2):
            start = pl.multiple_of(placed_piece(2 * tile + side, y, half) * PIECE, PIECE)
            adapter = adapter_scale * lax.dot_general(
                low[...], chosen[pl.ds(start, PIECE), :], rows, preferred_element_type=jnp.float32
            )
            piece = total[:, side * PIECE : (side + 1) * PIECE]
            at = pl.multiple_of(tile * TILE + side * PIECE, PIECE)
            out[:, pl.ds(at, PIECE)] = jnp.where(keep, piece, 0.0) + adapter


def late_kernel(where, half, early, *refs):
    meta, own, up1, dn1, up2, dn2, up3, dn3, low, chosen, sums = refs[:11]
    arrays, (out, cot, wbuf, csem, wsem) = refs[11:-5], refs[-5:]
    z, p, y, valid = meta[0], meta[1], meta[2], meta[3]
    depth, cols, tiles = wbuf.shape[0], own.shape[1], len(where)
    last = last_slot(z)

    def send(tile, slot):
        for side in range(2):
            for j in range(4):
                index, offset = where[tile][side][1][j]
                back = jnp.bitwise_and(z - jnp.bitwise_xor(p, j), 3)
                place = order_of(back, last)
                start_copy(
                    (back == last) if tile < early else (back >= 0),
                    arrays[index].at[offset],
                    wbuf.at[
                        slot,
                        pl.ds(side * PIECE, PIECE),
                        pl.ds(pl.multiple_of(place * cols, 128), cols),
                    ],
                    wsem.at[slot, side, place],
                )

    part = lambda place: cot.at[:, pl.ds(place * cols, cols)]
    start_copy(z == 0, dn3, part(3), csem.at[3])
    start_copy(z == 1, dn2, part(3), csem.at[3])
    start_copy(z == 2, up2, part(3), csem.at[3])
    start_copy(z == 3, up3, part(3), csem.at[3])
    for slot in range(depth - 1):
        send(slot, slot)
    start_copy(z >= 0, own, part(0), csem.at[0])
    start_copy(z == 0, dn2, part(1), csem.at[1])
    start_copy(z >= 1, up1, part(1), csem.at[1])
    start_copy(z <= 2, dn1, part(2), csem.at[2])
    start_copy(z == 3, up2, part(2), csem.at[2])
    keep = lax.broadcasted_iota(jnp.int32, (LIVE, 1), 0) < valid
    rows = (((1,), (1,)), ((), ()))
    out[LIVE:, :] = jnp.zeros((out.shape[0] - LIVE, out.shape[1]), out.dtype)
    pltpu.make_async_copy(part(3), part(3), csem.at[3]).wait()

    def product(tile, first):
        slot = lax.rem(tile, depth)
        for index in range(depth - 1, tiles):
            pl.when(tile + depth - 1 == index)(lambda index=index: send(index, index % depth))
        for side in range(2):
            for place in range(first, 4):
                target = wbuf.at[slot, pl.ds(side * PIECE, PIECE), pl.ds(place * cols, cols)]
                pltpu.make_async_copy(target, target, wsem.at[slot, side, place]).wait()
        return lax.dot_general(
            cot[:, first * cols :],
            wbuf[slot, :, first * cols :],
            rows,
            preferred_element_type=jnp.float32,
        )

    def store(tile, side, total, before):
        start = pl.multiple_of(placed_piece(2 * tile + side, y, half) * PIECE, PIECE)
        piece = jnp.where(keep, total[:, side * PIECE : (side + 1) * PIECE], 0.0)
        out[:LIVE, pl.ds(start, PIECE)] = (before(start) + piece).astype(out.dtype)

    @pl.loop(0, early)
    def _(tile):
        total = product(tile, 3)
        for side in range(2):
            at = pl.multiple_of(tile * TILE + side * PIECE, PIECE)
            store(tile, side, total, lambda start: sums[:, pl.ds(at, PIECE)])

    for place in range(3):
        pltpu.make_async_copy(part(place), part(place), csem.at[place]).wait()

    def adapter(start):
        return adapter_scale * lax.dot_general(
            low[...], chosen[pl.ds(start, PIECE), :], rows, preferred_element_type=jnp.float32
        )

    @pl.loop(early, tiles)
    def _(tile):
        total = product(tile, 0)
        for side in range(2):
            store(tile, side, total, adapter)


def matmul_call(kernel, out_shape, operands, vmem_count, scratch):
    smem = pl.BlockSpec(memory_space=pltpu.SMEM)
    vmem = pl.BlockSpec(memory_space=pltpu.VMEM)
    hbm = pl.BlockSpec(memory_space=pltpu.HBM)
    first, last = vmem_count
    specs = [smem] + [
        vmem if first <= i < last else hbm for i in range(1, len(operands))
    ]
    return pl.pallas_call(
        kernel,
        out_shape=out_shape,
        in_specs=specs,
        out_specs=vmem,
        scratch_shapes=scratch,
        compiler_params=pltpu.CompilerParams(vmem_limit_bytes=44 * 2**20),
        cost_estimate=pl.CostEstimate(flops=0, transcendentals=0, bytes_accessed=0),
    )(*operands)


def early_call(meta, low, chosen, near, arrays, where, half):
    cols, depth = near[0].shape[1], 3
    return matmul_call(
        lambda *refs: early_kernel(where, half, *refs),
        jax.ShapeDtypeStruct((LIVE, len(where) * TILE), jnp.float32),
        (meta, low, chosen, *near, *arrays),
        (1, 3),
        [
            pltpu.VMEM((LIVE, 3 * cols), jnp.bfloat16),
            pltpu.VMEM((depth, TILE, 3 * cols), jnp.bfloat16),
            pltpu.SemaphoreType.DMA((3,)),
            pltpu.SemaphoreType.DMA((depth, 2, 3)),
        ],
    )


def late_call(meta, near, low, chosen, sums, arrays, where, half, early, seq_len):
    cols, depth = near[0].shape[1], 3
    return matmul_call(
        lambda *refs: late_kernel(where, half, early, *refs),
        jax.ShapeDtypeStruct((seq_len, len(where) * TILE), jnp.bfloat16),
        (meta, *near, low, chosen, sums, *arrays),
        (1 + len(near), 4 + len(near)),
        [
            pltpu.VMEM((LIVE, 4 * cols), jnp.bfloat16),
            pltpu.VMEM((depth, TILE, 4 * cols), jnp.bfloat16),
            pltpu.SemaphoreType.DMA((4,)),
            pltpu.SemaphoreType.DMA((depth, 2, 4)),
        ],
    )


def gather_kernel(parts, *refs):
    inputs, (out, buffer, come, go) = refs[:-4], refs[-4:]
    moves = []
    for i, (index, source, target, size) in enumerate(parts):
        held = buffer.at[pl.ds(target, size)]
        arrive = pltpu.make_async_copy(inputs[index].at[pl.ds(source, size)], held, come.at[i])
        leave = pltpu.make_async_copy(held, out.at[pl.ds(target, size)], go.at[i])
        moves.append((arrive, leave))
        arrive.start()
    for arrive, leave in moves:
        arrive.wait()
        leave.start()
    for arrive, leave in moves:
        leave.wait()


def gather_call(arrays, parts, shape):
    spec = pl.BlockSpec(memory_space=pltpu.HBM)
    return pl.pallas_call(
        lambda *refs: gather_kernel(parts, *refs),
        out_shape=jax.ShapeDtypeStruct(shape, arrays[0].dtype),
        in_specs=[spec] * len(arrays),
        out_specs=spec,
        scratch_shapes=[
            pltpu.VMEM(shape, arrays[0].dtype),
            pltpu.SemaphoreType.DMA((len(parts),)),
            pltpu.SemaphoreType.DMA((len(parts),)),
        ],
        compiler_params=pltpu.CompilerParams(vmem_limit_bytes=32 * 2**20),
        cost_estimate=pl.CostEstimate(flops=0, transcendentals=0, bytes_accessed=0),
    )(*arrays)


def gather_pieces(arrays):
    parts = [(index, i) for index, array in enumerate(arrays) for i in range(array.shape[0])]
    moves = [(index, i, at, 1) for at, (index, i) in enumerate(parts)]
    return gather_call(arrays, moves, (len(moves),) + arrays[0].shape[1:])


def live_rows(array):
    size = LIVE // 8
    moves = [(0, i * size, i * size, size) for i in range(8)]
    return gather_call([array], moves, (LIVE, array.shape[1]))


def across(value):
    return lax.ppermute(value, "dp", [(i, i ^ 2) for i in range(4)])


def core(value):
    return lax.ppermute(value, "dp", [(i, i ^ 1) for i in range(4)])


def over(value):
    return lax.ppermute(value, "groups", [(0, 1), (1, 0)])


def line(value, step):
    def send(value, sign, far):
        pairs = [(i, i + 1) for i in range(far, 3)]
        return lax.ppermute(value, "fsdp", pairs if sign > 0 else [(3 - a, 3 - b) for a, b in pairs])

    return lambda sign: send(value, sign, step)


def turns(value):
    return [lax.ppermute(value, "fsdp", [(i, (i + k) % 4) for i in range(4)]) for k in (1, 2, 3)]


class Plan:
    def __init__(self, own, codes, scales, y):
        self.own, self.codes, self.scales = own, codes, scales.T
        self.pieces = codes.shape[0] // PIECE
        self.half = sum(SENT)
        self.group = y.astype(jnp.int32).reshape(1)
        self.up1, self.dn1 = line(own, 0)(1), line(own, 0)(-1)
        (head,) = weight_pieces(self.group, codes, self.scales, self.half, [(0, SENT[0])])
        self.x0 = across(head)

    def sum_parts(self, parts):
        spans = [(0, self.pieces), (SENT[0], self.half), (2 * self.half, self.pieces)]
        self.mine, first, self.direct = weight_pieces(
            after(self.group, parts), self.codes, self.scales, self.half, spans
        )
        gathered = lax.all_gather(after(parts, self.mine), "fsdp", axis=0)
        ready = (gathered, self.up1, self.dn1)
        self.x1 = across(after(first, *ready))
        self.y0 = over(after(self.x0, *ready))
        self.up2 = line(after(self.up1, *ready), 1)(1)
        self.dn2 = line(after(self.dn1, *ready), 1)(-1)
        self.sibling = core(after(self.mine, *ready, self.x0))
        return [gathered]

    def gather_rows(self, row):
        rows = lax.all_gather(row, "dp", axis=0, tiled=True)
        done = (self.x1, self.y0, self.up2, self.dn2, rows, self.sibling)
        self.y1 = over(after(self.x1, *done))
        self.x2 = across(after(self.direct, *done))
        self.up3 = line(after(self.up2, *done), 2)(1)
        self.dn3 = line(after(self.dn2, *done), 2)(-1)
        self.far1 = gather_pieces(after((self.x0, self.x1, self.y0), *done))
        self.sib_far1 = core(self.far1)
        return after([rows], self.sib_far1)

    def finish(self, done, state_part, meta, low, chosen, seq_len):
        half, sent = self.half, SENT[0]
        near = [self.own, self.up1, self.dn1, self.up2, self.dn2]
        arrays = [self.mine, self.sibling, self.far1, self.sib_far1]

        far_at = {i: (2, i) for i in range(half + sent)}
        far_at.update({half + sent + i: (4, i) for i in range(half - sent)})
        far_at.update({i: (6, i - 2 * half) for i in range(2 * half, self.pieces)})
        early_count = half + sent

        def entry(i):
            index, offset = far_at[i]
            return (i, ((0, i), (1, i), (index, offset), (index + 1, offset)))

        tiles = [(entry(i), entry(i + 1)) for i in range(0, self.pieces, 2)]
        early = early_count // 2
        sum1 = early_call(after(meta, done), low, chosen, near, arrays, tiles[:early], half)
        sib_y1 = core(after(self.y1, sum1))
        sib_x2 = core(after(self.x2, sib_y1, self.up3, self.dn3))
        others = turns(after(state_part, self.up3, self.dn3, sib_y1))
        arrays += [self.y1, sib_y1, self.x2, sib_x2]
        near += [self.up3, self.dn3]
        result = late_call(meta, near, low, chosen, sum1, arrays, tiles, half, early, seq_len)
        state_sum = state_part
        for other in others:
            state_sum = state_sum + after(other, result)
        return result, state_sum


def shards(
    hidden_in,
    cotangent,
    base_codes,
    base_scales,
    factor_a,
    factor_b,
    task_state,
    head_a,
    head_b,
    task_ids,
    valid_counts,
    owners,
):
    f32, bf16 = jnp.float32, jnp.bfloat16
    n_groups, n_fsdp, n_dp = (lax.axis_size(a) for a in ("groups", "fsdp", "dp"))
    z, p, y = (lax.axis_index(a) for a in ("fsdp", "dp", "groups"))
    seq_len, width_part = hidden_in.shape
    tasks_all, factor_cols = factor_a.shape
    rank_double = factor_cols // width_part
    rank_half = rank_double // 2
    joined_part = cotangent.shape[1]
    own = cotangent[:LIVE]
    lines = (n_groups, n_fsdp, n_dp) == (2, 4, 4) and width_part == 16 * PIECE
    own = live_rows(cotangent) if lines else own
    plan = Plan(own, base_codes, base_scales, y) if lines else None

    task_rows = lax.broadcasted_iota(jnp.int32, (tasks_all, tasks_all), 0)
    task_other = lax.broadcasted_iota(jnp.int32, (tasks_all, tasks_all), 1)
    same_owner = owners[:, None] == owners[None, :]
    slot_index = jnp.sum((same_owner & (task_other < task_rows)).astype(jnp.int32), axis=1)
    target = owners * SLOTS + slot_index

    task = task_ids[0]
    chosen_a = lax.dynamic_slice_in_dim(factor_a, task, 1, 0).reshape(width_part, rank_double)
    chosen_b = lax.dynamic_slice_in_dim(factor_b, task, 1, 0).reshape(joined_part, rank_half)
    first_column = (z * joined_part).astype(jnp.int32).reshape(1)
    parts = whole_call(
        product_kernel,
        jax.ShapeDtypeStruct((LIVE, 2 * rank_double), bf16),
        hidden_in,
        cotangent,
        chosen_a,
        chosen_b,
        scalars=(first_column,),
    )
    if lines:
        parts = plan.sum_parts(parts)
    else:
        parts = [lax.all_gather(parts, "fsdp", axis=0)]
    scalars = jnp.stack([first_column[0], valid_counts[0]])
    down_gradient, up_gradient, low_grad = whole_call(
        factor_kernel,
        [
            jax.ShapeDtypeStruct((width_part, rank_double), f32),
            jax.ShapeDtypeStruct((joined_part, rank_half), f32),
            jax.ShapeDtypeStruct((LIVE, rank_double), bf16),
        ],
        hidden_in,
        cotangent,
        *parts,
        scalars=(scalars,),
    )
    down_cols = width_part * rank_double
    up_cols = joined_part * rank_half
    row = whole_call(
        row_kernel,
        jax.ShapeDtypeStruct((1, down_cols + up_cols + 128), bf16),
        down_gradient.astype(bf16).reshape(1, down_cols),
        up_gradient.astype(bf16).reshape(1, up_cols),
        jnp.full((1, 128), task, f32).astype(bf16),
    )
    rows = plan.gather_rows(row) if lines else [lax.all_gather(row, "dp", axis=0, tiled=True)]
    ids = jnp.concatenate([row[:, down_cols + up_cols] for row in rows]).astype(jnp.int32)
    one_hot = ids[:, None] == lax.broadcasted_iota(jnp.int32, (1, tasks_all), 1)
    states = jnp.dot(one_hot.astype(bf16), task_state, preferred_element_type=f32).astype(bf16)
    block = math.gcd(down_cols, up_cols)
    grad_head_b, part_b = head_grads(states, rows, head_b, down_cols, block)
    if lines:
        rows = after(rows, grad_head_b)
    grad_head_a, part_a = head_grads(states, rows, head_a, 0, block)
    state_part = part_a + part_b
    seq_target = jnp.sum(jnp.where(one_hot, target[None, :], 0), axis=1)
    own_rows = z * SLOTS + lax.broadcasted_iota(jnp.int32, (SLOTS, 1), 0)
    selector = (own_rows == seq_target[None, :]).astype(f32)
    if lines:
        done = (grad_head_a, grad_head_b, selector)
        meta = jnp.stack([z, p, y, valid_counts[0]]).astype(jnp.int32)
        input_gradient, state_sum = plan.finish(
            done, state_part, meta, low_grad, chosen_a, seq_len
        )
    else:
        state_sum = jnp.sum(lax.all_gather(state_part, "fsdp", axis=0), axis=0)
    grad_state = jnp.sum(selector[:, :, None] * state_sum[None, :, :], axis=1)

    if not lines:
        weight = dequantize(
            lax.all_gather(base_codes, "dp", axis=1, tiled=True),
            lax.all_gather(base_scales, "dp", axis=1, tiled=True),
        )
        merged = lax.dot_general(
            lax.all_gather(own, "fsdp", axis=1, tiled=True),
            weight,
            (((1,), (1,)), ((), ())),
            preferred_element_type=f32,
        )
        adapter = lax.dot_general(
            low_grad, chosen_a, (((1,), (1,)), ((), ())), preferred_element_type=f32
        )
        keep = lax.broadcasted_iota(jnp.int32, (LIVE, 1), 0) < valid_counts[0]
        live = (jnp.where(keep, merged, 0.0) + adapter_scale * adapter).astype(bf16)
        input_gradient = jnp.pad(live, ((0, seq_len - LIVE), (0, 0)))
    return (input_gradient, grad_head_a, grad_head_b, grad_state)


def solution(mesh):
    placed = (
        P(("groups", "dp"), "fsdp"),
        P(("groups", "dp"), "fsdp"),
        P("fsdp", "dp"),
        P("fsdp", "dp"),
        P("groups", "fsdp"),
        P("groups", "fsdp"),
        P("groups", "dp"),
        P("dp", "fsdp"),
        P("dp", "fsdp"),
        P(("groups", "dp")),
        P(("groups", "dp")),
        P("groups"),
    )
    return jax.shard_map(
        shards,
        mesh=mesh,
        in_specs=placed,
        out_specs=(
            P(("groups", "dp"), "fsdp"),
            P(("groups", "dp"), "fsdp"),
            P(("groups", "dp"), "fsdp"),
            P(("groups", "fsdp"), "dp"),
        ),
        check_vma=False,
    )
```
